32 devices in a mesh: node: 8 (over z, x), local: 4 (over y, core).
Axes of the slice: x: 2, y: 2, z: 4, core: 2. Of those that a mesh axis runs over, the one named last changes fastest.
Arguments:
- tokens: bfloat16 [2048, 2048], P('node'), may hold values from -6 to 6
- expert_ids: int32 [2048, 8], P('node'), may hold values from 0 to 31, as said below
- gate_scores: float32 [2048, 8], P('node'), may hold values from 0.02 to 0.5
- expert_gate: bfloat16 [32, 2048, 768], P(('node', 'local')), may hold values from -0.125 to 0.125
- expert_up: bfloat16 [32, 2048, 768], P(('node', 'local')), may hold values from -0.125 to 0.125
- expert_down: bfloat16 [32, 768, 2048], P(('node', 'local')), may hold values from -0.21875 to 0.21875
- shared_gate: bfloat16 [2048, 2048], P(None, 'local'), may hold values from -0.125 to 0.125
- shared_up: bfloat16 [2048, 2048], P(None, 'local'), may hold values from -0.125 to 0.125
- shared_down: bfloat16 [2048, 2048], P('local'), may hold values from -0.125 to 0.125
Outputs:
- moe_out: bfloat16 [2048, 2048], P(('node', 'local'))
The draws below stay inside these ranges and needn't reach their ends.
Inputs may be any that keep to these rules, and one draw needn't show every extreme that they name: `expert_ids`: each token's 8 experts are distinct and lie in exactly 4 groups of 4 consecutive experts (group g is experts g * 4 to g * 4 + 3), two in each. Among the 256 tokens of one index of node, exactly 128 tokens pick experts in each group of 4 consecutive experts, no expert is picked by more than 128 tokens, and one expert is picked by exactly 128 of them in every such block.
All inputs are finite; a program needn't handle non-finite values.
Results may differ from the reference program's by a relative error of at most 0.015.
Values may be sent and summed in bfloat16 or wider, within the bound.
No kernel may reach another device: no remote copies, remote signals or barrier semaphores. Data moves between devices by JAX's collectives and lax.ppermute only.
A program may use at most 64 MiB of HBM per device.

```python
import math
import jax
import jax.numpy as jnp
from jax import lax

D = 2048
FF = 768
SH = 2048
E_NODE = 4
TOPK = 8
TOK_NODE = 256
EXPERTS = 32
SPLIT = 1
EXP_CAP = 128
TOKENS = 2048
N_NODE = 8


def draw_expert_ids(key, part):
    slot_count = TOPK // 2
    seq_length = slot_count * TOK_NODE
    least_run = -(-(seq_length - EXP_CAP) // (N_NODE - 1))
    key_list = jax.random.split(key, 3)
    hot_node = jax.random.randint(key_list[0], (), 0, N_NODE).astype(jnp.int32)
    hot_expert = jax.random.randint(key_list[1], (), 0, E_NODE).astype(jnp.int32)

    def draw_block(block_key):
        parts_keys = jax.random.split(block_key, 5)
        others = jax.random.permutation(parts_keys[0], N_NODE - 1).astype(jnp.int32)
        others = others + (others >= hot_node).astype(jnp.int32)
        node_order = jnp.concatenate([hot_node[None], others])
        run_lengths = jax.random.randint(parts_keys[1], (N_NODE,), least_run, EXP_CAP + 1).astype(jnp.int32)
        run_lengths = run_lengths.at[0].set(EXP_CAP)
        run_ends = jnp.cumsum(run_lengths)
        places = jnp.arange(seq_length, dtype=jnp.int32)
        which_run = jnp.sum((places[:, None] >= run_ends[None, :]).astype(jnp.int32), axis=1)
        sequence = node_order[which_run]
        nodes = sequence.reshape(slot_count, TOK_NODE).T
        token_perm = jax.random.permutation(parts_keys[2], TOK_NODE).astype(jnp.int32)
        nodes = nodes[token_perm]
        first_pick = jax.random.randint(parts_keys[3], (TOK_NODE, slot_count), 0, E_NODE).astype(jnp.int32)
        step_pick = jax.random.randint(parts_keys[4], (TOK_NODE, slot_count), 1, E_NODE).astype(jnp.int32)
        first_pick = jnp.where(nodes == hot_node, hot_expert, first_pick)
        second_pick = (first_pick + step_pick) % E_NODE
        pairs = jnp.stack([nodes * E_NODE + first_pick, nodes * E_NODE + second_pick], axis=-1)
        return pairs.reshape(TOK_NODE, TOPK)
    block_keys = jax.random.split(key_list[2], TOKENS // TOK_NODE)
    return jax.vmap(draw_block)(block_keys).reshape(TOKENS, TOPK).astype(jnp.int32)


def block_scale(own_key, shape, cuts, smallest, top_value):
    loudness = 1.0
    for dim, blocks in cuts:
        heights = jax.random.uniform(jax.random.fold_in(jax.random.fold_in(own_key, 6), dim), (blocks,), jnp.float32, smallest / len(cuts), top_value / len(cuts))
        loudness = loudness * jnp.repeat(jnp.exp(heights), shape[dim] // blocks).reshape((-1,) + (1,) * (len(shape) - 1 - dim))
    return loudness


def noise(key, dims, width, most, cuts=(), kind=jnp.bfloat16):
    values = width * jax.random.normal(key, dims, jnp.float32)
    if cuts:
        values = values * block_scale(key, dims, cuts, -0.22, 0.18)
    return jnp.clip(values, -most, most).astype(kind)


def setup_inputs(seed: int = 0) -> dict:
    seeds = jax.random.split(jax.random.key(seed), 10)
    tokens = noise(seeds[0], (TOKENS, D), 1.0, 6.0, ((0, 8),))
    expert_ids = draw_expert_ids(jax.random.fold_in(seeds[9], 71), 0)
    gate_scores = jnp.clip(jnp.exp(math.log(0.5) - 3.218876 * jax.random.uniform(seeds[2], (TOKENS, TOPK), jnp.float32) ** block_scale(seeds[2], (TOKENS, TOPK), ((0, 8),), -0.2, 0.2)), 0.02, 0.5)
    expert_gate = noise(seeds[3], (EXPERTS * SPLIT, D, FF // SPLIT), D ** -0.5, 0.125, ((0, 32),))
    expert_up = noise(seeds[4], (EXPERTS * SPLIT, D, FF // SPLIT), D ** -0.5, 0.125, ((0, 32),))
    expert_down = noise(seeds[5], (EXPERTS * SPLIT, FF // SPLIT, D), FF ** -0.5, 0.21875, ((0, 32),))
    shared_gate = noise(seeds[6], (D, SH), D ** -0.5, 0.125, ((1, 4),))
    shared_up = noise(seeds[7], (D, SH), D ** -0.5, 0.125, ((1, 4),))
    shared_down = noise(seeds[8], (SH, D), SH ** -0.5, 0.125, ((0, 4),))
    return {"tokens": tokens, "expert_ids": expert_ids, "gate_scores": gate_scores, "expert_gate": expert_gate, "expert_up": expert_up, "expert_down": expert_down, "shared_gate": shared_gate, "shared_up": shared_up, "shared_down": shared_down}


def reference(tokens, expert_ids, gate_scores, expert_gate, expert_up, expert_down, shared_gate, shared_up, shared_down):
    token_total = tokens.shape[0]
    max_rows = N_NODE * EXP_CAP
    shared_hidden = (jax.nn.silu(jnp.dot(tokens, shared_gate, preferred_element_type=jnp.float32))
                     * jnp.dot(tokens, shared_up, preferred_element_type=jnp.float32)).astype(jnp.bfloat16)
    shared_out = jnp.dot(shared_hidden, shared_down, preferred_element_type=jnp.float32)
    token_order = jnp.arange(token_total, dtype=jnp.int32)

    def add_expert(accumulated, expert):
        matches = expert_ids == expert
        picked = jnp.any(matches, axis=1)
        weights = jnp.sum(jnp.where(matches, gate_scores, jnp.zeros_like(gate_scores)), axis=1)
        position = jnp.cumsum(picked.astype(jnp.int32)) - 1
        destination = jnp.where(picked, position, max_rows).astype(jnp.int32)
        slot_token = jnp.zeros((max_rows,), jnp.int32).at[destination].set(token_order, mode="drop")
        slot_weight = jnp.zeros((max_rows,), gate_scores.dtype).at[destination].set(weights, mode="drop")
        rows = tokens[slot_token].astype(jnp.float32)
        first = (expert * SPLIT).astype(jnp.int32)
        gate_block = lax.dynamic_slice_in_dim(expert_gate, first, SPLIT, 0).astype(jnp.float32)
        up_block = lax.dynamic_slice_in_dim(expert_up, first, SPLIT, 0).astype(jnp.float32)
        down_block = lax.dynamic_slice_in_dim(expert_down, first, SPLIT, 0).astype(jnp.float32)
        gate_proj = jnp.einsum("rd,sdf->rsf", rows, gate_block)
        up_proj = jnp.einsum("rd,sdf->rsf", rows, up_block)
        hidden = (jax.nn.silu(gate_proj) * up_proj).astype(jnp.bfloat16)
        partial_value = jnp.einsum("rsf,sfd->rsd", hidden.astype(jnp.float32), down_block).astype(jnp.bfloat16)
        contrib = jnp.sum(partial_value.astype(jnp.float32), axis=1) * slot_weight[:, None]
        return accumulated.at[slot_token].add(contrib), None

    start_sum = jnp.zeros((token_total, tokens.shape[1]), jnp.float32)
    routed, _ = lax.scan(add_expert, start_sum, jnp.arange(EXPERTS, dtype=jnp.int32))
    return (shared_out + routed).astype(jnp.bfloat16)
```

```python
import functools

import jax
import jax.numpy as jnp
from jax import lax
from jax.experimental import pallas as pl
from jax.experimental.pallas import tpu as pltpu
from jax.sharding import PartitionSpec as P

E_NODE = 4
NEAR = 4
LANES = 128
VMEM_LIMIT = 40 * 1024 * 1024
F32 = jnp.float32
BF16 = jnp.bfloat16


def xor_node(x, k):
    count = lax.axis_size("node")
    return lax.ppermute(x, "node", [(i, i ^ k) for i in range(count)])


def xor_local(x, k):
    count = lax.axis_size("local")
    return lax.ppermute(x, "local", [(i, i ^ k) for i in range(count)])


def params():
    return pltpu.CompilerParams(vmem_limit_bytes=VMEM_LIMIT)


def cost(flops, nbytes, trans=0):
    return pl.CostEstimate(flops=int(flops), bytes_accessed=int(nbytes), transcendentals=int(trans))


SMEM = pl.BlockSpec(memory_space=pltpu.SMEM)
VMEM = pl.BlockSpec(memory_space=pltpu.VMEM)


def column_blocks(width, block=512):
    return [(c, min(block, width - c)) for c in range(0, width, block)]


def route_kernel(pieces, node_count, s_ref, ids_ref, score_ref, tok_ref, *refs):
    outs = refs[: len(pieces)]
    oh_ref, hot, rows = refs[len(pieces):]
    tok_rows, width = tok_ref.shape
    picks = ids_ref.shape[0]
    experts = node_count * E_NODE
    node = s_ref[0]
    ids = ids_ref[...]
    group = lax.div(ids, jnp.int32(E_NODE)) ^ node
    score = score_ref[...]
    group_iota = lax.broadcasted_iota(jnp.int32, (node_count, tok_rows), 0)
    expert_iota = lax.broadcasted_iota(jnp.int32, (experts, tok_rows), 0)
    member = jnp.zeros((node_count, tok_rows), F32)
    weight = jnp.zeros((experts, tok_rows), F32)
    for j in range(picks):
        member = jnp.where(group[j : j + 1] == group_iota, 1.0, member)
        weight = weight + jnp.where(ids[j : j + 1] == expert_iota, score[j : j + 1], 0.0)
    row = lax.broadcasted_iota(jnp.int32, (tok_rows, tok_rows), 0)
    col = lax.broadcasted_iota(jnp.int32, (tok_rows, tok_rows), 1)
    upper = jnp.where(row <= col, 1.0, 0.0).astype(BF16)
    position = jnp.dot(member.astype(BF16), upper, preferred_element_type=F32) - 1.0
    position = jnp.where(member > 0.0, position, -1.0).astype(jnp.int32)
    offset = 0
    for k, base, count in pieces:
        first = 0 if base is None else s_ref[base] * count
        slot = lax.broadcasted_iota(jnp.int32, (count, tok_rows), 0) + first
        hot[offset : offset + count, :] = jnp.where(position[k : k + 1] == slot, 1.0, 0.0)
        offset += count
    one_hot = hot[...].astype(BF16)
    oh_ref[...] = one_hot
    high = weight.astype(BF16)
    low = (weight - high.astype(F32)).astype(BF16)
    extra = outs[0].shape[1] - width
    parts = [high, low]
    if extra > 2 * experts:
        parts.append(jnp.zeros((extra - 2 * experts, tok_rows), BF16))
    table = jnp.concatenate(parts, axis=0)
    for c, w in column_blocks(width) + [(width, extra)]:
        if c < width:
            rows[:, :w] = jnp.dot(one_hot, tok_ref[:, c : c + w], preferred_element_type=F32)
        else:
            rows[:, :w] = lax.dot_general(one_hot, table, (((1,), (1,)), ((), ())), preferred_element_type=F32)
        offset = 0
        for out, (_, _, count) in zip(outs, pieces):
            out[:, c : c + w] = rows[offset : offset + count, :w].astype(BF16)
            offset += count


def route(scalars, ids, scores, tokens, pieces, node_count):
    tok_rows, width = tokens.shape
    experts = node_count * E_NODE
    full = width + -(-2 * experts // LANES) * LANES
    total = sum(p[2] for p in pieces)
    res = pl.pallas_call(
        functools.partial(route_kernel, pieces, node_count),
        out_shape=[jax.ShapeDtypeStruct((p[2], full), BF16) for p in pieces]
        + [jax.ShapeDtypeStruct((total, tok_rows), BF16)],
        in_specs=[SMEM, VMEM, VMEM, VMEM],
        out_specs=[VMEM] * (len(pieces) + 1),
        scratch_shapes=[pltpu.VMEM((total, tok_rows), F32), pltpu.VMEM((total, 512), F32)],
        compiler_params=params(),
        cost_estimate=cost(2 * total * tok_rows * full, 2 * (tok_rows * width + total * full)),
        name="route",
    )(scalars, ids, scores, tokens)
    return res[:-1], res[-1]


def ffn_kernel(counts, experts, keep_rows, s_ref, *refs):
    n = len(counts)
    xs = refs[:n]
    wg_ref, wu_ref, wd_ref = refs[n : n + 3]
    outs = refs[n + 3 : -3]
    x, acc, wcol = refs[-3:]
    width = x.shape[1]
    step = pl.program_id(0)

    @pl.when(step == 0)
    def _():
        expert = s_ref[2]
        extra = xs[0].shape[1] - width
        lane = lax.broadcasted_iota(jnp.int32, (1, extra), 1)
        mask = jnp.where((lane == expert) | (lane == expert + experts), 1.0, 0.0)
        offset = 0
        for ref, count in zip(xs, counts):
            x[offset : offset + count, :] = ref[:, :width].astype(x.dtype)
            wcol[offset : offset + count, :] = jnp.sum(ref[:, width:].astype(F32) * mask, axis=1, keepdims=True)
            offset += count

    rows = x[...].astype(BF16)
    gate = jnp.dot(rows, wg_ref[0], preferred_element_type=F32)
    up = jnp.dot(rows, wu_ref[0], preferred_element_type=F32)
    hidden = (jax.nn.silu(gate) * up).astype(BF16)
    for c, w in column_blocks(width):
        part = jnp.dot(hidden, wd_ref[0, :, c : c + w], preferred_element_type=F32)

        @pl.when(step == 0)
        def _():
            acc[:, c : c + w] = part

        @pl.when(step > 0)
        def _():
            acc[:, c : c + w] += part

    @pl.when(step == pl.num_programs(0) - 1)
    def _():
        total = acc.shape[0]
        outs[0][...] = (acc[:keep_rows] * wcol[:keep_rows]).astype(outs[0].dtype)
        if keep_rows < total:
            outs[1][...] = (acc[keep_rows:] * wcol[keep_rows:]).astype(outs[1].dtype)


def hidden_block(hidden):
    for size in (256, 128):
        if hidden % size == 0:
            return size
    return hidden


def ffn(scalars, xs, w_gate, w_up, w_down, experts, split):
    counts = [x.shape[0] for x in xs]
    total = sum(counts)
    width, hidden = w_gate.shape[1:]
    full = xs[0].shape[1]
    keep = total // 2 if split else total
    shapes = [jax.ShapeDtypeStruct((keep, width), F32 if split else BF16)]
    if split:
        shapes.append(jax.ShapeDtypeStruct((total - keep, width), BF16))
    block = hidden_block(hidden)
    whole = lambda count: pl.BlockSpec((count, full), lambda f: (0, 0))
    packed = all(c % 16 == 0 for c in counts)
    return pl.pallas_call(
        functools.partial(ffn_kernel, counts, experts, keep),
        grid=(hidden // block,),
        out_shape=shapes,
        in_specs=[SMEM]
        + [whole(c) for c in counts]
        + [
            pl.BlockSpec((1, width, block), lambda f: (0, 0, f)),
            pl.BlockSpec((1, width, block), lambda f: (0, 0, f)),
            pl.BlockSpec((1, block, width), lambda f: (0, f, 0)),
        ],
        out_specs=[pl.BlockSpec(s.shape, lambda f: (0, 0)) for s in shapes],
        scratch_shapes=[
            pltpu.VMEM((total, width), BF16 if packed else F32),
            pltpu.VMEM((total, width), F32),
            pltpu.VMEM((total, 1), F32),
        ],
        compiler_params=params(),
        cost_estimate=cost(6 * total * width * hidden, 6 * width * hidden + 6 * total * width, total * hidden),
        name="ffn",
    )(scalars, *xs, w_gate, w_up, w_down)


def shared_kernel(x_ref, wg_ref, wu_ref, wd_ref, out_ref):
    step = pl.program_id(0)
    rows = x_ref[...]
    gate = jnp.dot(rows, wg_ref[...], preferred_element_type=F32)
    up = jnp.dot(rows, wu_ref[...], preferred_element_type=F32)
    hidden = (jax.nn.silu(gate) * up).astype(BF16)
    for c, w in column_blocks(rows.shape[1]):
        part = jnp.dot(hidden, wd_ref[:, c : c + w], preferred_element_type=F32)

        @pl.when(step == 0)
        def _():
            out_ref[:, c : c + w] = part

        @pl.when(step > 0)
        def _():
            out_ref[:, c : c + w] += part


def shared(tokens, w_gate, w_up, w_down):
    rows, width = tokens.shape
    hidden = w_gate.shape[1]
    block = hidden_block(hidden)
    return pl.pallas_call(
        shared_kernel,
        grid=(hidden // block,),
        out_shape=jax.ShapeDtypeStruct((rows, width), F32),
        in_specs=[
            pl.BlockSpec((rows, width), lambda f: (0, 0)),
            pl.BlockSpec((width, block), lambda f: (0, f)),
            pl.BlockSpec((width, block), lambda f: (0, f)),
            pl.BlockSpec((block, width), lambda f: (f, 0)),
        ],
        out_specs=pl.BlockSpec((rows, width), lambda f: (0, 0)),
        compiler_params=params(),
        cost_estimate=cost(6 * rows * width * hidden, 6 * width * hidden + 6 * rows * width, rows * hidden),
        name="shared",
    )(tokens, w_gate, w_up, w_down)


def combine_kernel(counts, order, s_ref, oh_ref, shared_ref, *refs):
    n = len(counts)
    parts = refs[:n]
    keep_ref, send_ref, slots, acc = refs[n:]
    tok_rows, width = shared_ref.shape
    offset = 0
    for ref, count in zip(parts, counts):
        slots[offset : offset + count, :] = ref[...].astype(slots.dtype)
        offset += count
    one_hot = oh_ref[...]
    for c, w in column_blocks(width):
        acc[:, c : c + w] = lax.dot_general(
            one_hot, slots[:, c : c + w].astype(BF16), (((0,), (0,)), ((), ())), preferred_element_type=F32
        )
    block = tok_rows // len(order)
    half = len(order) // 2
    for j, rel in enumerate(order):
        start = pl.multiple_of((s_ref[1] ^ rel) * block, block)
        value = acc[pl.ds(start, block), :] + shared_ref[pl.ds(start, block), :]
        if j < half:
            keep_ref[j * block : (j + 1) * block, :] = value
        else:
            send_ref[(j - half) * block : (j - half + 1) * block, :] = value.astype(BF16)


def combine(scalars, one_hot, shared_part, parts, order):
    counts = [p.shape[0] for p in parts]
    tok_rows, width = shared_part.shape
    total = sum(counts)
    packed = all(c % 16 == 0 for c in counts)
    return pl.pallas_call(
        functools.partial(combine_kernel, counts, order),
        out_shape=[
            jax.ShapeDtypeStruct((tok_rows // 2, width), F32),
            jax.ShapeDtypeStruct((tok_rows // 2, width), BF16),
        ],
        in_specs=[SMEM] + [VMEM] * (len(parts) + 2),
        out_specs=[VMEM, VMEM],
        scratch_shapes=[
            pltpu.VMEM((total, width), BF16 if packed else F32),
            pltpu.VMEM((tok_rows, width), F32),
        ],
        compiler_params=params(),
        cost_estimate=cost(2 * total * tok_rows * width, 2 * total * width + 7 * tok_rows * width),
        name="combine",
    )(scalars, one_hot, shared_part, *parts)


def fold(value, bits):
    for bit in bits:
        half = value.shape[0] // 2
        value = value[:half] + xor_local(value[half:].astype(BF16), bit).astype(F32)
    return value


def far_chunks(node_count):
    top = node_count // 2
    chunks = []
    while top >= NEAR:
        chunks.append(list(range(top, 2 * top)))
        top //= 2
    if len(chunks) == 1 and len(chunks[0]) > 1:
        ks = chunks[0]
        chunks = [ks[len(ks) // 2 :], ks[: len(ks) // 2]]
    return chunks


def local(tokens, expert_ids, gate_scores, expert_gate, expert_up, expert_down, shared_gate, shared_up, shared_down):
    node_count = lax.axis_size("node")
    local_count = lax.axis_size("local")
    experts = node_count * E_NODE
    tok_rows, width = tokens.shape
    capacity = expert_ids.shape[1] * tok_rows // (2 * node_count)
    node = lax.axis_index("node")
    rank = lax.axis_index("local")
    own = node * E_NODE + rank // (local_count // E_NODE)
    scalars = jnp.stack([node, rank, own, rank % 2]).astype(jnp.int32)
    slow_bits = [1 << b for b in range(1, local_count.bit_length() - 1)]
    chunks = far_chunks(node_count)
    near = [k for k in range(1, NEAR)]
    pieces = [(k, 1, capacity // local_count) for ks in chunks for k in ks]
    pieces += [(k, 3, capacity // 2) for k in near] + [(0, None, capacity)]
    sends, one_hot = route(scalars, expert_ids.T, gate_scores.T, tokens, tuple(pieces), node_count)
    weights = (expert_gate, expert_up, expert_down)

    arrived = []
    index = 0
    for ks in chunks:
        arrived.append([xor_node(sends[index + i], k) for i, k in enumerate(ks)])
        index += len(ks)
    near_in = [xor_node(sends[index + i], k) for i, k in enumerate(near)]
    own_rows = sends[-1]

    shared_part = shared(tokens, shared_gate, shared_up, shared_down)
    own_out = ffn(scalars, [own_rows], *weights, experts, False)[0]

    def far_chunk(ks, got):
        rows = [jnp.concatenate(got, axis=0) if len(got) > 1 else got[0]]
        for bit in slow_bits:
            rows = rows + [xor_local(r, bit) for r in rows]
        rows = rows + [xor_local(r, 1) for r in rows]
        keep, send = ffn(scalars, rows, *weights, experts, True)
        value = keep + xor_local(send, 1).astype(F32)
        value = fold(value, slow_bits[::-1]).astype(BF16)
        count = value.shape[0] // len(ks)
        return [xor_node(value[i * count : (i + 1) * count], k) for i, k in enumerate(ks)]

    returned = far_chunk(chunks[0], arrived[0])
    near_rows = near_in + [xor_local(r, 1) for r in near_in]
    keep, send = ffn(scalars, near_rows, *weights, experts, True)
    near_sum = (keep + xor_local(send, 1).astype(F32)).astype(BF16)
    count = near_sum.shape[0] // len(near)
    near_back = [xor_node(near_sum[i * count : (i + 1) * count], k) for i, k in enumerate(near)]
    for ks, got in zip(chunks[1:], arrived[1:]):
        returned += far_chunk(ks, got)

    order = [0]
    for bit in slow_bits:
        order = order + [i ^ bit for i in order]
    order = order + [i ^ 1 for i in order]
    keep, send = combine(scalars, one_hot, shared_part, returned + near_back + [own_out], tuple(order))
    value = keep + xor_local(send, 1).astype(F32)
    return fold(value, slow_bits[::-1]).astype(BF16)


def solution(mesh):
    return jax.shard_map(
        local,
        mesh=mesh,
        in_specs=(
            P("node", None),
            P("node", None),
            P("node", None),
            P(("node", "local"), None, None),
            P(("node", "local"), None, None),
            P(("node", "local"), None, None),
            P(None, "local"),
            P(None, "local"),
            P("local", None),
        ),
        out_specs=P(("node", "local"), None),
        check_vma=False,
    )
```

```python
import functools

import jax
import jax.numpy as jnp
from jax import lax
from jax.experimental import pallas as pl
from jax.experimental.pallas import tpu as pltpu
from jax.sharding import PartitionSpec as P


E_NODE = 4
NEAR = 4
LANES = 128
VMEM_LIMIT = 24 * 1024 * 1024
F32 = jnp.float32
BF16 = jnp.bfloat16


def xor_node(x, k):
    count = lax.axis_size("node")
    return lax.ppermute(x, "node", [(i, i ^ k) for i in range(count)])


def xor_local(x, k):
    count = lax.axis_size("local")
    return lax.ppermute(x, "local", [(i, i ^ k) for i in range(count)])


def params():
    return pltpu.CompilerParams(vmem_limit_bytes=VMEM_LIMIT)


def cost(flops, nbytes, trans=0):
    return pl.CostEstimate(flops=int(flops), bytes_accessed=int(nbytes), transcendentals=int(trans))


SMEM = pl.BlockSpec(memory_space=pltpu.SMEM)
HBM = pl.BlockSpec(memory_space=pltpu.HBM)
VMEM = pl.BlockSpec(memory_space=pltpu.VMEM)


def column_blocks(width, block=512):
    return [(c, min(block, width - c)) for c in range(0, width, block)]


def route_kernel(pieces, node_count, s_ref, ids_hbm, score_hbm, tok_hbm, *refs):
    outs = refs[: len(pieces)]
    oh_ref, hot, rows, ids_ref, score_ref, tok_ref, sems = refs[len(pieces):]
    copies = [
        pltpu.make_async_copy(src, dst, sems.at[i])
        for i, (src, dst) in enumerate(((ids_hbm, ids_ref), (score_hbm, score_ref), (tok_hbm, tok_ref)))
    ]
    for copy in copies:
        copy.start()
    copies[0].wait()
    copies[1].wait()
    tok_rows, width = tok_ref.shape
    picks = ids_ref.shape[0]
    experts = node_count * E_NODE
    node = s_ref[0]
    ids = ids_ref[...]
    group = lax.div(ids, jnp.int32(E_NODE)) ^ node
    score = score_ref[...]
    group_iota = lax.broadcasted_iota(jnp.int32, (node_count, tok_rows), 0)
    expert_iota = lax.broadcasted_iota(jnp.int32, (experts, tok_rows), 0)
    member = jnp.zeros((node_count, tok_rows), F32)
    weight = jnp.zeros((experts, tok_rows), F32)
    for j in range(picks):
        member = jnp.where(group[j : j + 1] == group_iota, 1.0, member)
        weight = weight + jnp.where(ids[j : j + 1] == expert_iota, score[j : j + 1], 0.0)
    row = lax.broadcasted_iota(jnp.int32, (tok_rows, tok_rows), 0)
    col = lax.broadcasted_iota(jnp.int32, (tok_rows, tok_rows), 1)
    upper = jnp.where(row <= col, 1.0, 0.0).astype(BF16)
    position = jnp.dot(member.astype(BF16), upper, preferred_element_type=F32) - 1.0
    position = jnp.where(member > 0.0, position, -1.0).astype(jnp.int32)
    offset = 0
    for k, base, count in pieces:
        first = 0 if base is None else s_ref[base] * count
        slot = lax.broadcasted_iota(jnp.int32, (count, tok_rows), 0) + first
        hot[offset : offset + count, :] = jnp.where(position[k : k + 1] == slot, 1.0, 0.0)
        offset += count
    one_hot = hot[...].astype(BF16)
    oh_ref[...] = one_hot
    high = weight.astype(BF16)
    low = (weight - high.astype(F32)).astype(BF16)
    extra = outs[0].shape[1] - width
    parts = [high, low]
    if extra > 2 * experts:
        parts.append(jnp.zeros((extra - 2 * experts, tok_rows), BF16))
    table = jnp.concatenate(parts, axis=0)
    copies[2].wait()
    for c, w in column_blocks(width) + [(width, extra)]:
        if c < width:
            rows[:, :w] = jnp.dot(one_hot, tok_ref[:, c : c + w], preferred_element_type=F32)
        else:
            rows[:, :w] = lax.dot_general(one_hot, table, (((1,), (1,)), ((), ())), preferred_element_type=F32)
        offset = 0
        for out, (_, _, count) in zip(outs, pieces):
            out[:, c : c + w] = rows[offset : offset + count, :w].astype(BF16)
            offset += count


def route(scalars, ids, scores, tokens, pieces, node_count):
    tok_rows, width = tokens.shape
    experts = node_count * E_NODE
    full = width + -(-2 * experts // LANES) * LANES
    total = sum(p[2] for p in pieces)
    res = pl.pallas_call(
        functools.partial(route_kernel, pieces, node_count),
        out_shape=[jax.ShapeDtypeStruct((p[2], full), BF16) for p in pieces]
        + [jax.ShapeDtypeStruct((total, tok_rows), BF16)],
        in_specs=[SMEM, HBM, HBM, HBM],
        out_specs=[VMEM] * (len(pieces) + 1),
        scratch_shapes=[
            pltpu.VMEM((total, tok_rows), F32),
            pltpu.VMEM((total, 512), F32),
            pltpu.VMEM(ids.shape, ids.dtype),
            pltpu.VMEM(scores.shape, scores.dtype),
            pltpu.VMEM(tokens.shape, tokens.dtype),
            pltpu.SemaphoreType.DMA((3,)),
        ],
        compiler_params=params(),
        cost_estimate=cost(2 * total * tok_rows * full, 2 * (tok_rows * width + total * full)),
        name="route",
    )(scalars, ids, scores, tokens)
    return res[:-1], res[-1]


def hidden_block(hidden):
    for size in (256, 128):
        if hidden % size == 0:
            return size
    return hidden


def ffn_kernel(counts, experts, keep_rows, s_ref, *refs):
    n = len(counts)
    xs = refs[:n]
    wg_ref, wu_ref, wd_ref = refs[n : n + 3]
    outs = refs[n + 3 : -2]
    x, wcol = refs[-2:]
    total, width = x.shape
    expert = s_ref[2]
    extra = xs[0].shape[1] - width
    lane = lax.broadcasted_iota(jnp.int32, (1, extra), 1)
    mask = jnp.where((lane == expert) | (lane == expert + experts), 1.0, 0.0)
    offset = 0
    for ref, count in zip(xs, counts):
        x[offset : offset + count, :] = ref[:, :width].astype(x.dtype)
        wcol[offset : offset + count, :] = jnp.sum(ref[:, width:].astype(F32) * mask, axis=1, keepdims=True)
        offset += count
    rows = x[...].astype(BF16)
    hidden = []
    for c, w in column_blocks(wg_ref.shape[2], 256):
        gate = jnp.dot(rows, wg_ref[0, :, c : c + w], preferred_element_type=F32)
        up = jnp.dot(rows, wu_ref[0, :, c : c + w], preferred_element_type=F32)
        hidden.append((jax.nn.silu(gate) * up).astype(BF16))
    hidden = jnp.concatenate(hidden, axis=1) if len(hidden) > 1 else hidden[0]
    scale = wcol[...]
    for c, w in column_blocks(width):
        part = jnp.dot(hidden, wd_ref[0, :, c : c + w], preferred_element_type=F32) * scale
        outs[0][:, c : c + w] = part[:keep_rows].astype(outs[0].dtype)
        if keep_rows < total:
            outs[1][:, c : c + w] = part[keep_rows:].astype(outs[1].dtype)


def ffn(scalars, xs, w_gate, w_up, w_down, experts, split):
    counts = [x.shape[0] for x in xs]
    total = sum(counts)
    width, hidden = w_gate.shape[1:]
    keep = total // 2 if split else total
    shapes = [jax.ShapeDtypeStruct((keep, width), F32 if split else BF16)]
    if split:
        shapes.append(jax.ShapeDtypeStruct((total - keep, width), BF16))
    packed = all(c % 16 == 0 for c in counts)
    return pl.pallas_call(
        functools.partial(ffn_kernel, counts, experts, keep),
        out_shape=shapes,
        in_specs=[SMEM] + [VMEM] * (len(xs) + 3),
        out_specs=[VMEM] * len(shapes),
        scratch_shapes=[
            pltpu.VMEM((total, width), BF16 if packed else F32),
            pltpu.VMEM((total, 1), F32),
        ],
        compiler_params=params(),
        cost_estimate=cost(6 * total * width * hidden, 6 * width * hidden + 6 * total * width, total * hidden),
    )(scalars, *xs, w_gate, w_up, w_down)


def shared_kernel(x_ref, wg_ref, wu_ref, wd_ref, eg_hbm, eu_hbm, ed_hbm, out_ref, eg_ref, eu_ref, ed_ref, sems):
    step = pl.program_id(0)
    staged = [
        pltpu.make_async_copy(src, dst, sems.at[i])
        for i, (src, dst) in enumerate(((eg_hbm, eg_ref), (eu_hbm, eu_ref), (ed_hbm, ed_ref)))
    ]

    @pl.when(step == 0)
    def _():
        for copy in staged:
            copy.start()

    rows = x_ref[...]
    gate = jnp.dot(rows, wg_ref[...], preferred_element_type=F32)
    up = jnp.dot(rows, wu_ref[...], preferred_element_type=F32)
    hidden = (jax.nn.silu(gate) * up).astype(BF16)
    for c, w in column_blocks(rows.shape[1]):
        part = jnp.dot(hidden, wd_ref[:, c : c + w], preferred_element_type=F32)

        @pl.when(step == 0)
        def _():
            out_ref[:, c : c + w] = part

        @pl.when(step > 0)
        def _():
            out_ref[:, c : c + w] += part

    @pl.when(step == pl.num_programs(0) - 1)
    def _():
        for copy in staged:
            copy.wait()


def shared(tokens, w_gate, w_up, w_down, staged):
    rows, width = tokens.shape
    hidden = w_gate.shape[1]
    block = hidden_block(hidden)
    return pl.pallas_call(
        shared_kernel,
        grid=(hidden // block,),
        out_shape=[jax.ShapeDtypeStruct((rows, width), F32)] + [jax.ShapeDtypeStruct(w.shape, w.dtype) for w in staged],
        in_specs=[
            pl.BlockSpec((rows, width), lambda f: (0, 0)),
            pl.BlockSpec((width, block), lambda f: (0, f)),
            pl.BlockSpec((width, block), lambda f: (0, f)),
            pl.BlockSpec((block, width), lambda f: (f, 0)),
            HBM,
            HBM,
            HBM,
        ],
        out_specs=[pl.BlockSpec((rows, width), lambda f: (0, 0)), VMEM, VMEM, VMEM],
        scratch_shapes=[pltpu.SemaphoreType.DMA((3,))],
        compiler_params=params(),
        cost_estimate=cost(
            6 * rows * width * hidden,
            6 * width * hidden + 6 * rows * width + sum(4 * w.size for w in staged),
            rows * hidden,
        ),
        name="shared",
    )(tokens, w_gate, w_up, w_down, *staged)


def combine_kernel(counts, order, s_ref, oh_ref, shared_ref, *refs):
    n = len(counts)
    parts = refs[:n]
    keep_ref, send_ref, slots, acc = refs[n:]
    tok_rows, width = shared_ref.shape
    offset = 0
    for ref, count in zip(parts, counts):
        slots[offset : offset + count, :] = ref[...].astype(slots.dtype)
        offset += count
    one_hot = oh_ref[...]
    for c, w in column_blocks(width):
        acc[:, c : c + w] = lax.dot_general(
            one_hot, slots[:, c : c + w].astype(BF16), (((0,), (0,)), ((), ())), preferred_element_type=F32
        )
    block = tok_rows // len(order)
    half = len(order) // 2
    for j, rel in enumerate(order):
        start = pl.multiple_of((s_ref[1] ^ rel) * block, block)
        value = acc[pl.ds(start, block), :] + shared_ref[pl.ds(start, block), :]
        if j < half:
            keep_ref[j * block : (j + 1) * block, :] = value
        else:
            send_ref[(j - half) * block : (j - half + 1) * block, :] = value.astype(BF16)


def combine(scalars, one_hot, shared_part, parts, order):
    counts = [p.shape[0] for p in parts]
    tok_rows, width = shared_part.shape
    total = sum(counts)
    packed = all(c % 16 == 0 for c in counts)
    return pl.pallas_call(
        functools.partial(combine_kernel, counts, order),
        out_shape=[
            jax.ShapeDtypeStruct((tok_rows // 2, width), F32),
            jax.ShapeDtypeStruct((tok_rows // 2, width), BF16),
        ],
        in_specs=[SMEM] + [VMEM] * (len(parts) + 2),
        out_specs=[VMEM, VMEM],
        scratch_shapes=[
            pltpu.VMEM((total, width), BF16 if packed else F32),
            pltpu.VMEM((tok_rows, width), F32),
        ],
        compiler_params=params(),
        cost_estimate=cost(2 * total * tok_rows * width, 2 * total * width + 7 * tok_rows * width),
        name="combine",
    )(scalars, one_hot, shared_part, *parts)


def fold(value, bits):
    for bit in bits:
        half = value.shape[0] // 2
        value = value[:half] + xor_local(value[half:].astype(BF16), bit).astype(F32)
    return value


def far_chunks(node_count):
    top = node_count // 2
    chunks = []
    while top >= NEAR:
        chunks.append(list(range(top, 2 * top)))
        top //= 2
    if len(chunks) == 1 and len(chunks[0]) > 1:
        ks = chunks[0]
        chunks = [ks[len(ks) // 2 :], ks[: len(ks) // 2]]
    return chunks


def local(tokens, expert_ids, gate_scores, expert_gate, expert_up, expert_down, shared_gate, shared_up, shared_down):
    node_count = lax.axis_size("node")
    local_count = lax.axis_size("local")
    experts = node_count * E_NODE
    tok_rows, _ = tokens.shape
    capacity = expert_ids.shape[1] * tok_rows // (2 * node_count)
    node = lax.axis_index("node")
    rank = lax.axis_index("local")
    own = node * E_NODE + rank // (local_count // E_NODE)
    scalars = jnp.stack([node, rank, own, rank % 2]).astype(jnp.int32)
    slow_bits = [1 << b for b in range(1, local_count.bit_length() - 1)]
    chunks = far_chunks(node_count)
    near = [k for k in range(1, NEAR)]
    pieces = [(k, 1, capacity // local_count) for ks in chunks for k in ks]
    pieces += [(k, 3, capacity // 2) for k in near] + [(0, None, capacity)]
    sends, one_hot = route(scalars, expert_ids.T, gate_scores.T, tokens, tuple(pieces), node_count)
    weights = (expert_gate, expert_up, expert_down)

    arrived = []
    index = 0
    for ks in chunks:
        got = []
        for k in ks:
            got.append(xor_node(sends[index], k))
            index += 1
        arrived.append(got)
    near_in = []
    for k in near:
        near_in.append(xor_node(sends[index], k))
        index += 1
    own_rows = sends[-1]

    shared_part, *weights = shared(tokens, shared_gate, shared_up, shared_down, weights)
    own_out = ffn(scalars, [own_rows], *weights, experts, False)[0]

    def gather(got):
        rows = [jnp.concatenate(got, axis=0) if len(got) > 1 else got[0]]
        for bit in slow_bits:
            rows = rows + [xor_local(r, bit) for r in rows]
        return rows + [xor_local(r, 1) for r in rows]

    def experts_of(rows):
        keep, send = ffn(scalars, rows, *weights, experts, True)
        return keep + xor_local(send, 1).astype(F32)

    near_rows = near_in + [xor_local(r, 1) for r in near_in]
    near_sum = experts_of(near_rows).astype(BF16)
    count = near_sum.shape[0] // len(near)
    near_back = []
    for i, k in enumerate(near):
        near_back.append(xor_node(near_sum[i * count : (i + 1) * count], k))
    returned = []
    for ks, got in zip(chunks, arrived):
        value = experts_of(gather(got))
        value = fold(value, slow_bits[::-1]).astype(BF16)
        count = value.shape[0] // len(ks)
        for i, k in enumerate(ks):
            returned.append(xor_node(value[i * count : (i + 1) * count], k))

    order = [0]
    for bit in slow_bits:
        order = order + [i ^ bit for i in order]
    order = order + [i ^ 1 for i in order]
    keep, send = combine(scalars, one_hot, shared_part, returned + near_back + [own_out], tuple(order))
    value = keep + xor_local(send, 1).astype(F32)
    return fold(value, slow_bits[::-1]).astype(BF16)


def solution(mesh):
    return shard(mesh)


def shard(mesh):
    return jax.shard_map(
        local,
        mesh=mesh,
        in_specs=(
            P("node", None),
            P("node", None),
            P("node", None),
            P(("node", "local"), None, None),
            P(("node", "local"), None, None),
            P(("node", "local"), None, None),
            P(None, "local"),
            P(None, "local"),
            P("local", None),
        ),
        out_specs=P(("node", "local"), None),
        check_vma=False,
    )
```

```python
import functools

import jax
import jax.numpy as jnp
from jax import lax
from jax.experimental import pallas as pl
from jax.experimental.pallas import tpu as pltpu
from jax.sharding import PartitionSpec as P


E_NODE = 4
NEAR = 4
LANES = 128
VMEM_LIMIT = 24 * 1024 * 1024
F32 = jnp.float32
BF16 = jnp.bfloat16


def xor_node(x, k):
    count = lax.axis_size("node")
    return lax.ppermute(x, "node", [(i, i ^ k) for i in range(count)])


def xor_local(x, k):
    count = lax.axis_size("local")
    return lax.ppermute(x, "local", [(i, i ^ k) for i in range(count)])


def params():
    return pltpu.CompilerParams(vmem_limit_bytes=VMEM_LIMIT)


def cost(flops, nbytes, trans=0):
    return pl.CostEstimate(flops=int(flops), bytes_accessed=int(nbytes), transcendentals=int(trans))


SMEM = pl.BlockSpec(memory_space=pltpu.SMEM)
HBM = pl.BlockSpec(memory_space=pltpu.HBM)
VMEM = pl.BlockSpec(memory_space=pltpu.VMEM)


def column_blocks(width, block=512):
    return [(c, min(block, width - c)) for c in range(0, width, block)]


def route_kernel(pieces, node_count, s_ref, ids_hbm, score_hbm, tok_hbm, *refs):
    outs = refs[: len(pieces)]
    oh_ref, hot, rows, ids_ref, score_ref, tok_ref, sems = refs[len(pieces):]
    copies = [
        pltpu.make_async_copy(src, dst, sems.at[i])
        for i, (src, dst) in enumerate(((ids_hbm, ids_ref), (score_hbm, score_ref), (tok_hbm, tok_ref)))
    ]
    for copy in copies:
        copy.start()
    copies[0].wait()
    copies[1].wait()
    tok_rows, width = tok_ref.shape
    picks = ids_ref.shape[0]
    experts = node_count * E_NODE
    node = s_ref[0]
    ids = ids_ref[...]
    group = lax.div(ids, jnp.int32(E_NODE)) ^ node
    score = score_ref[...]
    group_iota = lax.broadcasted_iota(jnp.int32, (node_count, tok_rows), 0)
    expert_iota = lax.broadcasted_iota(jnp.int32, (experts, tok_rows), 0)
    member = jnp.zeros((node_count, tok_rows), F32)
    weight = jnp.zeros((experts, tok_rows), F32)
    for j in range(picks):
        member = jnp.where(group[j : j + 1] == group_iota, 1.0, member)
        weight = weight + jnp.where(ids[j : j + 1] == expert_iota, score[j : j + 1], 0.0)
    row = lax.broadcasted_iota(jnp.int32, (tok_rows, tok_rows), 0)
    col = lax.broadcasted_iota(jnp.int32, (tok_rows, tok_rows), 1)
    upper = jnp.where(row <= col, 1.0, 0.0).astype(BF16)
    position = jnp.dot(member.astype(BF16), upper, preferred_element_type=F32) - 1.0
    position = jnp.where(member > 0.0, position, -1.0).astype(jnp.int32)
    offset = 0
    for k, base, count in pieces:
        first = 0 if base is None else s_ref[base] * count
        slot = lax.broadcasted_iota(jnp.int32, (count, tok_rows), 0) + first
        hot[offset : offset + count, :] = jnp.where(position[k : k + 1] == slot, 1.0, 0.0)
        offset += count
    one_hot = hot[...].astype(BF16)
    oh_ref[...] = one_hot
    high = weight.astype(BF16)
    low = (weight - high.astype(F32)).astype(BF16)
    extra = outs[0].shape[1] - width
    parts = [high, low]
    if extra > 2 * experts:
        parts.append(jnp.zeros((extra - 2 * experts, tok_rows), BF16))
    table = jnp.concatenate(parts, axis=0)
    copies[2].wait()
    for c, w in column_blocks(width) + [(width, extra)]:
        if c < width:
            rows[:, :w] = jnp.dot(one_hot, tok_ref[:, c : c + w], preferred_element_type=F32)
        else:
            rows[:, :w] = lax.dot_general(one_hot, table, (((1,), (1,)), ((), ())), preferred_element_type=F32)
        offset = 0
        for out, (_, _, count) in zip(outs, pieces):
            out[:, c : c + w] = rows[offset : offset + count, :w].astype(BF16)
            offset += count


def route(scalars, ids, scores, tokens, pieces, node_count):
    tok_rows, width = tokens.shape
    experts = node_count * E_NODE
    full = width + -(-2 * experts // LANES) * LANES
    total = sum(p[2] for p in pieces)
    res = pl.pallas_call(
        functools.partial(route_kernel, pieces, node_count),
        out_shape=[jax.ShapeDtypeStruct((p[2], full), BF16) for p in pieces]
        + [jax.ShapeDtypeStruct((total, tok_rows), BF16)],
        in_specs=[SMEM, HBM, HBM, HBM],
        out_specs=[VMEM] * (len(pieces) + 1),
        scratch_shapes=[
            pltpu.VMEM((total, tok_rows), F32),
            pltpu.VMEM((total, 512), F32),
            pltpu.VMEM(ids.shape, ids.dtype),
            pltpu.VMEM(scores.shape, scores.dtype),
            pltpu.VMEM(tokens.shape, tokens.dtype),
            pltpu.SemaphoreType.DMA((3,)),
        ],
        compiler_params=params(),
        cost_estimate=cost(2 * total * tok_rows * full, 2 * (tok_rows * width + total * full)),
        name="route",
    )(scalars, ids, scores, tokens)
    return res[:-1], res[-1]


def hidden_block(hidden):
    for size in (256, 128):
        if hidden % size == 0:
            return size
    return hidden


def ffn_kernel(counts, experts, keep_rows, s_ref, *refs):
    n = len(counts)
    xs = refs[:n]
    wg_ref, wu_ref, wd_ref = refs[n : n + 3]
    outs = refs[n + 3 : -2]
    x, wcol = refs[-2:]
    total, width = x.shape
    expert = s_ref[2]
    extra = xs[0].shape[1] - width
    lane = lax.broadcasted_iota(jnp.int32, (1, extra), 1)
    mask = jnp.where((lane == expert) | (lane == expert + experts), 1.0, 0.0)
    offset = 0
    for ref, count in zip(xs, counts):
        x[offset : offset + count, :] = ref[:, :width].astype(x.dtype)
        wcol[offset : offset + count, :] = jnp.sum(ref[:, width:].astype(F32) * mask, axis=1, keepdims=True)
        offset += count
    rows = x[...].astype(BF16)
    hidden = []
    for c, w in column_blocks(wg_ref.shape[2], 256):
        gate = jnp.dot(rows, wg_ref[0, :, c : c + w], preferred_element_type=F32)
        up = jnp.dot(rows, wu_ref[0, :, c : c + w], preferred_element_type=F32)
        hidden.append((jax.nn.silu(gate) * up).astype(BF16))
    hidden = jnp.concatenate(hidden, axis=1) if len(hidden) > 1 else hidden[0]
    scale = wcol[...]
    for c, w in column_blocks(width):
        part = jnp.dot(hidden, wd_ref[0, :, c : c + w], preferred_element_type=F32) * scale
        outs[0][:, c : c + w] = part[:keep_rows].astype(outs[0].dtype)
        if keep_rows < total:
            outs[1][:, c : c + w] = part[keep_rows:].astype(outs[1].dtype)


def ffn(scalars, xs, w_gate, w_up, w_down, experts, split):
    counts = [x.shape[0] for x in xs]
    total = sum(counts)
    width, hidden = w_gate.shape[1:]
    keep = total // 2 if split else total
    shapes = [jax.ShapeDtypeStruct((keep, width), F32 if split else BF16)]
    if split:
        shapes.append(jax.ShapeDtypeStruct((total - keep, width), BF16))
    packed = all(c % 16 == 0 for c in counts)
    return pl.pallas_call(
        functools.partial(ffn_kernel, counts, experts, keep),
        out_shape=shapes,
        in_specs=[SMEM] + [VMEM] * (len(xs) + 3),
        out_specs=[VMEM] * len(shapes),
        scratch_shapes=[
            pltpu.VMEM((total, width), BF16 if packed else F32),
            pltpu.VMEM((total, 1), F32),
        ],
        compiler_params=params(),
        cost_estimate=cost(6 * total * width * hidden, 6 * width * hidden + 6 * total * width, total * hidden),
    )(scalars, *xs, w_gate, w_up, w_down)


def shared_kernel(x_ref, wg_ref, wu_ref, wd_ref, eg_hbm, eu_hbm, ed_hbm, out_ref, eg_ref, eu_ref, ed_ref, sems):
    step = pl.program_id(0)
    staged = [
        pltpu.make_async_copy(src, dst, sems.at[i])
        for i, (src, dst) in enumerate(((eg_hbm, eg_ref), (eu_hbm, eu_ref), (ed_hbm, ed_ref)))
    ]

    @pl.when(step == 0)
    def _():
        for copy in staged:
            copy.start()

    rows = x_ref[...]
    gate = jnp.dot(rows, wg_ref[...], preferred_element_type=F32)
    up = jnp.dot(rows, wu_ref[...], preferred_element_type=F32)
    hidden = (jax.nn.silu(gate) * up).astype(BF16)
    for c, w in column_blocks(rows.shape[1]):
        part = jnp.dot(hidden, wd_ref[:, c : c + w], preferred_element_type=F32)

        @pl.when(step == 0)
        def _():
            out_ref[:, c : c + w] = part

        @pl.when(step > 0)
        def _():
            out_ref[:, c : c + w] += part

    @pl.when(step == pl.num_programs(0) - 1)
    def _():
        for copy in staged:
            copy.wait()


def shared(tokens, w_gate, w_up, w_down, staged):
    rows, width = tokens.shape
    hidden = w_gate.shape[1]
    block = hidden_block(hidden)
    return pl.pallas_call(
        shared_kernel,
        grid=(hidden // block,),
        out_shape=[jax.ShapeDtypeStruct((rows, width), F32)] + [jax.ShapeDtypeStruct(w.shape, w.dtype) for w in staged],
        in_specs=[
            pl.BlockSpec((rows, width), lambda f: (0, 0)),
            pl.BlockSpec((width, block), lambda f: (0, f)),
            pl.BlockSpec((width, block), lambda f: (0, f)),
            pl.BlockSpec((block, width), lambda f: (f, 0)),
            HBM,
            HBM,
            HBM,
        ],
        out_specs=[pl.BlockSpec((rows, width), lambda f: (0, 0)), VMEM, VMEM, VMEM],
        scratch_shapes=[pltpu.SemaphoreType.DMA((3,))],
        compiler_params=params(),
        cost_estimate=cost(
            6 * rows * width * hidden,
            6 * width * hidden + 6 * rows * width + sum(4 * w.size for w in staged),
            rows * hidden,
        ),
        name="shared",
    )(tokens, w_gate, w_up, w_down, *staged)


def combine_kernel(counts, order, s_ref, oh_ref, shared_ref, *refs):
    n = len(counts)
    parts = refs[:n]
    keep_ref, send_ref, slots, acc = refs[n:]
    tok_rows, width = shared_ref.shape
    offset = 0
    for ref, count in zip(parts, counts):
        slots[offset : offset + count, :] = ref[...].astype(slots.dtype)
        offset += count
    one_hot = oh_ref[...]
    for c, w in column_blocks(width):
        acc[:, c : c + w] = lax.dot_general(
            one_hot, slots[:, c : c + w].astype(BF16), (((0,), (0,)), ((), ())), preferred_element_type=F32
        )
    block = tok_rows // len(order)
    half = len(order) // 2
    for j, rel in enumerate(order):
        start = pl.multiple_of((s_ref[1] ^ rel) * block, block)
        value = acc[pl.ds(start, block), :] + shared_ref[pl.ds(start, block), :]
        if j < half:
            keep_ref[j * block : (j + 1) * block, :] = value
        else:
            send_ref[(j - half) * block : (j - half + 1) * block, :] = value.astype(BF16)


def combine(scalars, one_hot, shared_part, parts, order):
    counts = [p.shape[0] for p in parts]
    tok_rows, width = shared_part.shape
    total = sum(counts)
    packed = all(c % 16 == 0 for c in counts)
    return pl.pallas_call(
        functools.partial(combine_kernel, counts, order),
        out_shape=[
            jax.ShapeDtypeStruct((tok_rows // 2, width), F32),
            jax.ShapeDtypeStruct((tok_rows // 2, width), BF16),
        ],
        in_specs=[SMEM] + [VMEM] * (len(parts) + 2),
        out_specs=[VMEM, VMEM],
        scratch_shapes=[
            pltpu.VMEM((total, width), BF16 if packed else F32),
            pltpu.VMEM((tok_rows, width), F32),
        ],
        compiler_params=params(),
        cost_estimate=cost(2 * total * tok_rows * width, 2 * total * width + 7 * tok_rows * width),
        name="combine",
    )(scalars, one_hot, shared_part, *parts)


def fold(value, bits):
    for bit in bits:
        half = value.shape[0] // 2
        value = value[:half] + xor_local(value[half:].astype(BF16), bit).astype(F32)
    return value


def far_chunks(node_count):
    top = node_count // 2
    chunks = []
    while top >= NEAR:
        chunks.append(list(range(top, 2 * top)))
        top //= 2
    if len(chunks) == 1 and len(chunks[0]) > 1:
        ks = chunks[0]
        chunks = [ks[len(ks) // 2 :], ks[: len(ks) // 2]]
    return chunks


def local(tokens, expert_ids, gate_scores, expert_gate, expert_up, expert_down, shared_gate, shared_up, shared_down):
    node_count = lax.axis_size("node")
    local_count = lax.axis_size("local")
    experts = node_count * E_NODE
    tok_rows, _ = tokens.shape
    capacity = expert_ids.shape[1] * tok_rows // (2 * node_count)
    node = lax.axis_index("node")
    rank = lax.axis_index("local")
    own = node * E_NODE + rank // (local_count // E_NODE)
    scalars = jnp.stack([node, rank, own, rank % 2]).astype(jnp.int32)
    slow_bits = [1 << b for b in range(1, local_count.bit_length() - 1)]
    chunks = far_chunks(node_count)
    near = [k for k in range(1, NEAR)]
    pieces = [(k, 1, capacity // local_count) for ks in chunks for k in ks]
    pieces += [(k, 3, capacity // 2) for k in near] + [(0, None, capacity)]
    in_hbm = functools.partial(pltpu.with_memory_space_constraint, memory_space=pltpu.HBM)
    sends, one_hot = route(
        scalars, in_hbm(expert_ids.T), in_hbm(gate_scores.T), in_hbm(tokens), tuple(pieces), node_count
    )
    weights = [pltpu.with_memory_space_constraint(w, pltpu.HBM) for w in (expert_gate, expert_up, expert_down)]
    shared_gate, shared_up, shared_down = [
        pltpu.with_memory_space_constraint(w, pltpu.HBM) for w in (shared_gate, shared_up, shared_down)
    ]

    arrived = []
    index = 0
    for ks in chunks:
        got = []
        for k in ks:
            got.append(xor_node(sends[index], k))
            index += 1
        arrived.append(got)
    near_in = []
    for k in near:
        near_in.append(xor_node(sends[index], k))
        index += 1
    own_rows = sends[-1]

    shared_part, *weights = shared(tokens, shared_gate, shared_up, shared_down, weights)
    own_out = ffn(scalars, [own_rows], *weights, experts, False)[0]

    def gather(got):
        rows = [jnp.concatenate(got, axis=0) if len(got) > 1 else got[0]]
        for bit in slow_bits:
            rows = rows + [xor_local(r, bit) for r in rows]
        return rows + [xor_local(r, 1) for r in rows]

    def experts_of(rows):
        keep, send = ffn(scalars, rows, *weights, experts, True)
        return keep + xor_local(send, 1).astype(F32)

    near_rows = near_in + [xor_local(r, 1) for r in near_in]
    near_sum = experts_of(near_rows).astype(BF16)
    count = near_sum.shape[0] // len(near)
    near_back = []
    for i, k in enumerate(near):
        near_back.append(xor_node(near_sum[i * count : (i + 1) * count], k))
    returned = []
    for ks, got in zip(chunks, arrived):
        value = experts_of(gather(got))
        value = fold(value, slow_bits[::-1]).astype(BF16)
        count = value.shape[0] // len(ks)
        for i, k in enumerate(ks):
            returned.append(xor_node(value[i * count : (i + 1) * count], k))

    order = [0]
    for bit in slow_bits:
        order = order + [i ^ bit for i in order]
    order = order + [i ^ 1 for i in order]
    keep, send = combine(scalars, one_hot, shared_part, returned + near_back + [own_out], tuple(order))
    value = keep + xor_local(send, 1).astype(F32)
    return fold(value, slow_bits[::-1]).astype(BF16)


def solution(mesh):
    return shard(mesh)


def shard(mesh):
    return jax.shard_map(
        local,
        mesh=mesh,
        in_specs=(
            P("node", None),
            P("node", None),
            P("node", None),
            P(("node", "local"), None, None),
            P(("node", "local"), None, None),
            P(("node", "local"), None, None),
            P(None, "local"),
            P(None, "local"),
            P("local", None),
        ),
        out_specs=P(("node", "local"), None),
        check_vma=False,
    )
```

```python
import functools

import jax
import jax.numpy as jnp
from jax import lax
from jax.experimental import pallas as pl
from jax.experimental.pallas import tpu as pltpu
from jax.sharding import PartitionSpec as P


E_NODE = 4
NEAR = 4
LANES = 128
VMEM_LIMIT = 24 * 1024 * 1024
F32 = jnp.float32
BF16 = jnp.bfloat16


def xor_node(x, k):
    count = lax.axis_size("node")
    return lax.ppermute(x, "node", [(i, i ^ k) for i in range(count)])


def xor_local(x, k):
    count = lax.axis_size("local")
    return lax.ppermute(x, "local", [(i, i ^ k) for i in range(count)])


def params():
    return pltpu.CompilerParams(vmem_limit_bytes=VMEM_LIMIT)


def cost(flops, nbytes, trans=0):
    return pl.CostEstimate(flops=int(flops), bytes_accessed=int(nbytes), transcendentals=int(trans))


SMEM = pl.BlockSpec(memory_space=pltpu.SMEM)
HBM = pl.BlockSpec(memory_space=pltpu.HBM)
VMEM = pl.BlockSpec(memory_space=pltpu.VMEM)


def column_blocks(width, block=512):
    return [(c, min(block, width - c)) for c in range(0, width, block)]


def route_kernel(pieces, node_count, s_ref, ids_hbm, score_hbm, tok_hbm, *refs):
    outs = refs[: len(pieces)]
    late_ref, early_ref, hot, rows, ids_ref, score_ref, tok_ref, sems = refs[len(pieces):]
    copies = [
        pltpu.make_async_copy(src, dst, sems.at[i])
        for i, (src, dst) in enumerate(((ids_hbm, ids_ref), (score_hbm, score_ref), (tok_hbm, tok_ref)))
    ]
    for copy in copies:
        copy.start()
    copies[0].wait()
    copies[1].wait()
    tok_rows, width = tok_ref.shape
    picks = ids_ref.shape[0]
    experts = node_count * E_NODE
    node = s_ref[0]
    ids = ids_ref[...]
    group = lax.div(ids, jnp.int32(E_NODE)) ^ node
    score = score_ref[...]
    group_iota = lax.broadcasted_iota(jnp.int32, (node_count, tok_rows), 0)
    expert_iota = lax.broadcasted_iota(jnp.int32, (experts, tok_rows), 0)
    member = jnp.zeros((node_count, tok_rows), F32)
    weight = jnp.zeros((experts, tok_rows), F32)
    for j in range(picks):
        member = jnp.where(group[j : j + 1] == group_iota, 1.0, member)
        weight = weight + jnp.where(ids[j : j + 1] == expert_iota, score[j : j + 1], 0.0)
    row = lax.broadcasted_iota(jnp.int32, (tok_rows, tok_rows), 0)
    col = lax.broadcasted_iota(jnp.int32, (tok_rows, tok_rows), 1)
    upper = jnp.where(row <= col, 1.0, 0.0).astype(BF16)
    position = jnp.dot(member.astype(BF16), upper, preferred_element_type=F32) - 1.0
    position = jnp.where(member > 0.0, position, -1.0).astype(jnp.int32)
    offset = 0
    for k, base, count in pieces:
        first = 0 if base is None else s_ref[base] * count
        slot = lax.broadcasted_iota(jnp.int32, (count, tok_rows), 0) + first
        hot[offset : offset + count, :] = jnp.where(position[k : k + 1] == slot, 1.0, 0.0)
        offset += count
    one_hot = hot[...].astype(BF16)
    split = late_ref.shape[0]
    late_ref[...] = hot[:split, :].astype(BF16)
    early_ref[...] = hot[split:, :].astype(BF16)
    high = weight.astype(BF16)
    low = (weight - high.astype(F32)).astype(BF16)
    extra = outs[0].shape[1] - width
    parts = [high, low]
    if extra > 2 * experts:
        parts.append(jnp.zeros((extra - 2 * experts, tok_rows), BF16))
    table = jnp.concatenate(parts, axis=0)
    copies[2].wait()
    for c, w in column_blocks(width) + [(width, extra)]:
        if c < width:
            rows[:, :w] = jnp.dot(one_hot, tok_ref[:, c : c + w], preferred_element_type=F32)
        else:
            rows[:, :w] = lax.dot_general(one_hot, table, (((1,), (1,)), ((), ())), preferred_element_type=F32)
        offset = 0
        for out, (_, _, count) in zip(outs, pieces):
            out[:, c : c + w] = rows[offset : offset + count, :w].astype(BF16)
            offset += count


def route(scalars, ids, scores, tokens, pieces, node_count):
    tok_rows, width = tokens.shape
    experts = node_count * E_NODE
    full = width + -(-2 * experts // LANES) * LANES
    total = sum(p[2] for p in pieces)
    tail = sum(p[2] for p in pieces[-2:])
    res = pl.pallas_call(
        functools.partial(route_kernel, pieces, node_count),
        out_shape=[jax.ShapeDtypeStruct((p[2], full), BF16) for p in pieces]
        + [jax.ShapeDtypeStruct((count, tok_rows), BF16) for count in (total - tail, tail)],
        in_specs=[SMEM, HBM, HBM, HBM],
        out_specs=[VMEM] * (len(pieces) + 2),
        scratch_shapes=[
            pltpu.VMEM((total, tok_rows), F32),
            pltpu.VMEM((total, 512), F32),
            pltpu.VMEM(ids.shape, ids.dtype),
            pltpu.VMEM(scores.shape, scores.dtype),
            pltpu.VMEM(tokens.shape, tokens.dtype),
            pltpu.SemaphoreType.DMA((3,)),
        ],
        compiler_params=params(),
        cost_estimate=cost(2 * total * tok_rows * full, 2 * (tok_rows * width + total * full)),
        name="route",
    )(scalars, ids, scores, tokens)
    return res[:-2], res[-2], res[-1]


def hidden_block(hidden):
    for size in (256, 128):
        if hidden % size == 0:
            return size
    return hidden


def ffn_kernel(counts, experts, ranges, s_ref, *refs):
    n = len(counts)
    xs = refs[:n]
    wg_ref, wu_ref, wd_ref = refs[n : n + 3]
    outs = refs[n + 3 : -2]
    x, wcol = refs[-2:]
    _, width = x.shape
    expert = s_ref[2]
    extra = xs[0].shape[1] - width
    lane = lax.broadcasted_iota(jnp.int32, (1, extra), 1)
    mask = jnp.where((lane == expert) | (lane == expert + experts), 1.0, 0.0)
    offset = 0
    for ref, count in zip(xs, counts):
        x[offset : offset + count, :] = ref[:, :width].astype(x.dtype)
        wcol[offset : offset + count, :] = jnp.sum(ref[:, width:].astype(F32) * mask, axis=1, keepdims=True)
        offset += count
    rows = x[...].astype(BF16)
    hidden = []
    for c, w in column_blocks(wg_ref.shape[2], 256):
        gate = jnp.dot(rows, wg_ref[0, :, c : c + w], preferred_element_type=F32)
        up = jnp.dot(rows, wu_ref[0, :, c : c + w], preferred_element_type=F32)
        hidden.append((jax.nn.silu(gate) * up).astype(BF16))
    hidden = jnp.concatenate(hidden, axis=1) if len(hidden) > 1 else hidden[0]
    scale = wcol[...]
    for c, w in column_blocks(width):
        part = jnp.dot(hidden, wd_ref[0, :, c : c + w], preferred_element_type=F32) * scale
        for out, (first, last) in zip(outs, ranges):
            out[:, c : c + w] = part[first:last].astype(out.dtype)


def ffn(scalars, xs, w_gate, w_up, w_down, experts, groups):
    counts = [x.shape[0] for x in xs]
    total = sum(counts)
    width, hidden = w_gate.shape[1:]
    shapes, ranges, done = [], [], 0
    for number, dtype in groups:
        first = sum(counts[:done])
        done += number
        ranges.append((first, sum(counts[:done])))
        shapes.append(jax.ShapeDtypeStruct((ranges[-1][1] - first, width), dtype))
    packed = all(c % 16 == 0 for c in counts)
    return pl.pallas_call(
        functools.partial(ffn_kernel, counts, experts, ranges),
        out_shape=shapes,
        in_specs=[SMEM] + [VMEM] * (len(xs) + 3),
        out_specs=[VMEM] * len(shapes),
        scratch_shapes=[
            pltpu.VMEM((total, width), BF16 if packed else F32),
            pltpu.VMEM((total, 1), F32),
        ],
        compiler_params=params(),
        cost_estimate=cost(6 * total * width * hidden, 6 * width * hidden + 6 * total * width, total * hidden),
    )(scalars, *xs, w_gate, w_up, w_down)


def stage_kernel(*refs):
    count = len(refs) // 2
    sems = refs[-1]
    copies = [pltpu.make_async_copy(refs[i], refs[count + i], sems.at[i]) for i in range(count)]
    for copy in copies:
        copy.start()
    for copy in copies:
        copy.wait()


def stage(weights):
    return pl.pallas_call(
        stage_kernel,
        out_shape=[jax.ShapeDtypeStruct(w.shape, w.dtype) for w in weights],
        in_specs=[HBM] * len(weights),
        out_specs=[VMEM] * len(weights),
        scratch_shapes=[pltpu.SemaphoreType.DMA((len(weights),))],
        compiler_params=params(),
        cost_estimate=cost(0, sum(4 * w.size for w in weights)),
        name="stage",
    )(*weights)


def shared_kernel(x_ref, wg_ref, wu_ref, wd_ref, out_ref):
    step = pl.program_id(0)
    rows = x_ref[...]
    gate = jnp.dot(rows, wg_ref[...], preferred_element_type=F32)
    up = jnp.dot(rows, wu_ref[...], preferred_element_type=F32)
    hidden = (jax.nn.silu(gate) * up).astype(BF16)
    for c, w in column_blocks(rows.shape[1]):
        part = jnp.dot(hidden, wd_ref[:, c : c + w], preferred_element_type=F32)

        @pl.when(step == 0)
        def _():
            out_ref[:, c : c + w] = part

        @pl.when(step > 0)
        def _():
            out_ref[:, c : c + w] += part


def shared(tokens, w_gate, w_up, w_down):
    rows, width = tokens.shape
    hidden = w_gate.shape[1]
    block = hidden_block(hidden)
    return pl.pallas_call(
        shared_kernel,
        grid=(hidden // block,),
        out_shape=jax.ShapeDtypeStruct((rows, width), F32),
        in_specs=[
            pl.BlockSpec((rows, width), lambda f: (0, 0)),
            pl.BlockSpec((width, block), lambda f: (0, f)),
            pl.BlockSpec((width, block), lambda f: (0, f)),
            pl.BlockSpec((block, width), lambda f: (f, 0)),
        ],
        out_specs=pl.BlockSpec((rows, width), lambda f: (0, 0)),
        compiler_params=params(),
        cost_estimate=cost(6 * rows * width * hidden, 6 * width * hidden + 6 * rows * width, rows * hidden),
        name="shared",
    )(tokens, w_gate, w_up, w_down)


def token_blocks(acc, order, s_ref):
    rows = acc.shape[0] // len(order)
    for j, rel in enumerate(order):
        start = pl.multiple_of((s_ref[1] ^ rel) * rows, rows)
        yield j, j * rows, acc[pl.ds(start, rows), :]


def gathered(oh_ref, parts, counts, slots, acc):
    offset = 0
    for ref, count in zip(parts, counts):
        slots[offset : offset + count, :] = ref[...].astype(slots.dtype)
        offset += count
    for c, w in column_blocks(acc.shape[1]):
        acc[:, c : c + w] = lax.dot_general(
            oh_ref[...], slots[:, c : c + w].astype(BF16), (((0,), (0,)), ((), ())), preferred_element_type=F32
        )


def early_kernel(counts, order, s_ref, oh_ref, shared_ref, *refs):
    n = len(counts)
    out_ref, slots, acc = refs[n:]
    gathered(oh_ref, refs[:n], counts, slots, acc)
    acc[...] = acc[...] + shared_ref[...]
    for j, at, value in token_blocks(acc, order, s_ref):
        out_ref[at : at + value.shape[0], :] = value


def combine_kernel(counts, order, s_ref, oh_ref, base_ref, *refs):
    n = len(counts)
    keep_ref, send_ref, slots, acc = refs[n:]
    gathered(oh_ref, refs[:n], counts, slots, acc)
    kept = keep_ref.shape[0]
    for j, at, value in token_blocks(acc, order, s_ref):
        value = value + base_ref[at : at + value.shape[0], :]
        if at < kept:
            keep_ref[at : at + value.shape[0], :] = value
        else:
            send_ref[at - kept : at - kept + value.shape[0], :] = value.astype(BF16)


def combine(scalars, one_hot, base, parts, order, final):
    counts = [p.shape[0] for p in parts]
    tok_rows, width = base.shape
    total = sum(counts)
    packed = all(c % 16 == 0 for c in counts)
    if final:
        shapes = [jax.ShapeDtypeStruct((tok_rows // 2, width), t) for t in (F32, BF16)]
    else:
        shapes = [jax.ShapeDtypeStruct((tok_rows, width), F32)]
    return pl.pallas_call(
        functools.partial(combine_kernel if final else early_kernel, counts, order),
        out_shape=shapes,
        in_specs=[SMEM] + [VMEM] * (len(parts) + 2),
        out_specs=[VMEM] * len(shapes),
        scratch_shapes=[
            pltpu.VMEM((total, width), BF16 if packed else F32),
            pltpu.VMEM((tok_rows, width), F32),
        ],
        compiler_params=params(),
        cost_estimate=cost(2 * total * tok_rows * width, 2 * total * width + 7 * tok_rows * width),
    )(scalars, one_hot, base, *parts)


def fold(value, bits):
    for bit in bits:
        half = value.shape[0] // 2
        value = value[:half] + xor_local(value[half:].astype(BF16), bit).astype(F32)
    return value


def far_chunks(node_count):
    top = node_count // 2
    chunks = []
    while top >= NEAR:
        chunks.append(list(range(top, 2 * top)))
        top //= 2
    if len(chunks) == 1 and len(chunks[0]) > 1:
        ks = chunks[0]
        chunks = [ks[len(ks) // 2 :], ks[: len(ks) // 2]]
    return chunks


def local(tokens, expert_ids, gate_scores, expert_gate, expert_up, expert_down, shared_gate, shared_up, shared_down):
    node_count = lax.axis_size("node")
    local_count = lax.axis_size("local")
    experts = node_count * E_NODE
    tok_rows, _ = tokens.shape
    capacity = expert_ids.shape[1] * tok_rows // (2 * node_count)
    node = lax.axis_index("node")
    rank = lax.axis_index("local")
    own = node * E_NODE + rank // (local_count // E_NODE)
    scalars = jnp.stack([node, rank, own, rank % 2]).astype(jnp.int32)
    slow_bits = [1 << b for b in range(1, local_count.bit_length() - 1)]
    chunks = far_chunks(node_count)
    near = [k for k in range(1, NEAR)]
    pieces = [(k, 1, capacity // local_count) for ks in chunks for k in ks]
    pieces += [(k, 3, capacity // 2) for k in near[1:] + near[:1]] + [(0, None, capacity)]
    in_hbm = functools.partial(pltpu.with_memory_space_constraint, memory_space=pltpu.HBM)
    sends, late_hot, early_hot = route(
        scalars, in_hbm(expert_ids.T), in_hbm(gate_scores.T), in_hbm(tokens), tuple(pieces), node_count
    )
    weights = [pltpu.with_memory_space_constraint(w, pltpu.HBM) for w in (expert_gate, expert_up, expert_down)]
    shared_gate, shared_up, shared_down = [
        pltpu.with_memory_space_constraint(w, pltpu.HBM) for w in (shared_gate, shared_up, shared_down)
    ]

    arrived = []
    index = 0
    for ks in chunks:
        got = []
        for k in ks:
            got.append(xor_node(sends[index], k))
            index += 1
        arrived.append(got)
    near_in = []
    for k in near[1:] + near[:1]:
        near_in.append(xor_node(sends[index], k))
        index += 1
    near_in = near_in[-1:] + near_in[:-1]
    own_rows = sends[-1]

    shared_part = shared(in_hbm(tokens), shared_gate, shared_up, shared_down)
    weights = stage(weights)

    def gather(got):
        rows = [jnp.concatenate(got, axis=0) if len(got) > 1 else got[0]]
        for bit in slow_bits:
            rows = rows + [xor_local(r, bit) for r in rows]
        return rows + [xor_local(r, 1) for r in rows]

    def summed(keep, send):
        return keep + xor_local(send, 1).astype(F32)

    def experts_of(rows):
        half = len(rows) // 2
        keep, send = ffn(scalars, rows, *weights, experts, ((half, F32), (half, BF16)))
        return summed(keep, send)

    partner = xor_local(near_in[0], 1)
    rows = [own_rows, near_in[0], partner]
    own_out, keep, send = ffn(scalars, rows, *weights, experts, ((1, BF16), (1, F32), (1, BF16)))
    near_sum = summed(keep, send).astype(BF16)
    near_back = [xor_node(near_sum, 1)]

    near_rows = near_in[1:] + [xor_local(r, 1) for r in near_in[1:]]
    near_sum = experts_of(near_rows).astype(BF16)
    count = near_sum.shape[0] // len(near_in[1:])
    for i, k in enumerate(near[1:]):
        near_back.append(xor_node(near_sum[i * count : (i + 1) * count], k))
    returned = []
    for ks, got in zip(chunks, arrived):
        value = experts_of(gather(got))
        value = fold(value, slow_bits[::-1]).astype(BF16)
        count = value.shape[0] // len(ks)
        for i, k in enumerate(ks):
            returned.append(xor_node(value[i * count : (i + 1) * count], k))

    order = [0]
    for bit in slow_bits:
        order = order + [i ^ bit for i in order]
    order = order + [i ^ 1 for i in order]
    base = combine(scalars, early_hot, shared_part, [near_back[0], own_out], tuple(order), False)[0]
    parts = returned + near_back[1:]
    keep, send = combine(scalars, late_hot, base, parts, tuple(order), True)
    value = keep + xor_local(send, 1).astype(F32)
    return fold(value, slow_bits[::-1]).astype(BF16)


def solution(mesh):
    return shard(mesh)


def shard(mesh):
    return jax.shard_map(
        local,
        mesh=mesh,
        in_specs=(
            P("node", None),
            P("node", None),
            P("node", None),
            P(("node", "local"), None, None),
            P(("node", "local"), None, None),
            P(("node", "local"), None, None),
            P(None, "local"),
            P(None, "local"),
            P("local", None),
        ),
        out_specs=P(("node", "local"), None),
        check_vma=False,
    )
```

```python
import functools

import jax
import jax.numpy as jnp
from jax import lax
from jax.experimental import pallas as pl
from jax.experimental.pallas import tpu as pltpu
from jax.sharding import PartitionSpec as P


E_NODE = 4
NEAR = 4
LANES = 128
VMEM_LIMIT = 24 * 1024 * 1024
F32 = jnp.float32
BF16 = jnp.bfloat16


def xor_node(x, k):
    count = lax.axis_size("node")
    return lax.ppermute(x, "node", [(i, i ^ k) for i in range(count)])


def xor_local(x, k):
    count = lax.axis_size("local")
    return lax.ppermute(x, "local", [(i, i ^ k) for i in range(count)])


def params():
    return pltpu.CompilerParams(vmem_limit_bytes=VMEM_LIMIT)


def cost(flops, nbytes, trans=0):
    return pl.CostEstimate(flops=int(flops), bytes_accessed=int(nbytes), transcendentals=int(trans))


SMEM = pl.BlockSpec(memory_space=pltpu.SMEM)
HBM = pl.BlockSpec(memory_space=pltpu.HBM)
VMEM = pl.BlockSpec(memory_space=pltpu.VMEM)


def column_blocks(width, block=512):
    return [(c, min(block, width - c)) for c in range(0, width, block)]


def route_kernel(pieces, node_count, s_ref, ids_hbm, score_hbm, tok_hbm, *refs):
    outs = refs[: len(pieces)]
    late_ref, early_ref, hot, rows, ids_ref, score_ref, tok_ref, sems = refs[len(pieces):]
    copies = [
        pltpu.make_async_copy(src, dst, sems.at[i])
        for i, (src, dst) in enumerate(((ids_hbm, ids_ref), (score_hbm, score_ref), (tok_hbm, tok_ref)))
    ]
    for copy in copies:
        copy.start()
    copies[0].wait()
    copies[1].wait()
    tok_rows, width = tok_ref.shape
    picks = ids_ref.shape[0]
    experts = node_count * E_NODE
    node = s_ref[0]
    ids = ids_ref[...]
    group = lax.div(ids, jnp.int32(E_NODE)) ^ node
    score = score_ref[...]
    group_iota = lax.broadcasted_iota(jnp.int32, (node_count, tok_rows), 0)
    expert_iota = lax.broadcasted_iota(jnp.int32, (experts, tok_rows), 0)
    member = jnp.zeros((node_count, tok_rows), F32)
    weight = jnp.zeros((experts, tok_rows), F32)
    for j in range(picks):
        member = jnp.where(group[j : j + 1] == group_iota, 1.0, member)
        weight = weight + jnp.where(ids[j : j + 1] == expert_iota, score[j : j + 1], 0.0)
    row = lax.broadcasted_iota(jnp.int32, (tok_rows, tok_rows), 0)
    col = lax.broadcasted_iota(jnp.int32, (tok_rows, tok_rows), 1)
    upper = jnp.where(row <= col, 1.0, 0.0).astype(BF16)
    position = jnp.dot(member.astype(BF16), upper, preferred_element_type=F32) - 1.0
    position = jnp.where(member > 0.0, position, -1.0).astype(jnp.int32)
    offset = 0
    for k, base, count in pieces:
        first = 0 if base is None else s_ref[base] * count
        slot = lax.broadcasted_iota(jnp.int32, (count, tok_rows), 0) + first
        hot[offset : offset + count, :] = jnp.where(position[k : k + 1] == slot, 1.0, 0.0)
        offset += count
    one_hot = hot[...].astype(BF16)
    split = late_ref.shape[0]
    late_ref[...] = hot[:split, :].astype(BF16)
    early_ref[...] = hot[split:, :].astype(BF16)
    high = weight.astype(BF16)
    low = (weight - high.astype(F32)).astype(BF16)
    extra = outs[0].shape[1] - width
    parts = [high, low]
    if extra > 2 * experts:
        parts.append(jnp.zeros((extra - 2 * experts, tok_rows), BF16))
    table = jnp.concatenate(parts, axis=0)
    copies[2].wait()
    aligned = all(count % 16 == 0 for _, _, count in pieces)
    for c, w in column_blocks(width) + [(width, extra)]:
        if c < width:
            value = jnp.dot(one_hot, tok_ref[:, c : c + w], preferred_element_type=F32)
        else:
            value = lax.dot_general(one_hot, table, (((1,), (1,)), ((), ())), preferred_element_type=F32)
        if not aligned:
            rows[:, :w] = value
            value = rows
        offset = 0
        for out, (_, _, count) in zip(outs, pieces):
            out[:, c : c + w] = value[offset : offset + count, :w].astype(BF16)
            offset += count


def route(scalars, ids, scores, tokens, pieces, node_count):
    tok_rows, width = tokens.shape
    experts = node_count * E_NODE
    full = width + -(-2 * experts // LANES) * LANES
    total = sum(p[2] for p in pieces)
    tail = sum(p[2] for p in pieces[-2:])
    res = pl.pallas_call(
        functools.partial(route_kernel, pieces, node_count),
        out_shape=[jax.ShapeDtypeStruct((p[2], full), BF16) for p in pieces]
        + [jax.ShapeDtypeStruct((count, tok_rows), BF16) for count in (total - tail, tail)],
        in_specs=[SMEM, HBM, HBM, HBM],
        out_specs=[VMEM] * (len(pieces) + 2),
        scratch_shapes=[
            pltpu.VMEM((total, tok_rows), F32),
            pltpu.VMEM((total, 512), F32),
            pltpu.VMEM(ids.shape, ids.dtype),
            pltpu.VMEM(scores.shape, scores.dtype),
            pltpu.VMEM(tokens.shape, tokens.dtype),
            pltpu.SemaphoreType.DMA((3,)),
        ],
        compiler_params=params(),
        cost_estimate=cost(2 * total * tok_rows * full, 2 * (tok_rows * width + total * full)),
        name="route",
    )(scalars, ids, scores, tokens)
    return res[:-2], res[-2], res[-1]


def hidden_block(hidden):
    for size in (256, 128):
        if hidden % size == 0:
            return size
    return hidden


def ffn_kernel(counts, experts, ranges, s_ref, *refs):
    n = len(counts)
    xs = refs[:n]
    wg_ref, wu_ref, wd_ref = refs[n : n + 3]
    outs = refs[n + 3 : -2]
    x, wcol = refs[-2:]
    _, width = x.shape
    expert = s_ref[2]
    extra = xs[0].shape[1] - width
    lane = lax.broadcasted_iota(jnp.int32, (1, extra), 1)
    mask = jnp.where((lane == expert) | (lane == expert + experts), 1.0, 0.0)
    offset = 0
    for ref, count in zip(xs, counts):
        x[offset : offset + count, :] = ref[:, :width].astype(x.dtype)
        wcol[offset : offset + count, :] = jnp.sum(ref[:, width:].astype(F32) * mask, axis=1, keepdims=True)
        offset += count
    rows = x[...].astype(BF16)
    hidden = []
    for c, w in column_blocks(wg_ref.shape[2], 256):
        gate = jnp.dot(rows, wg_ref[0, :, c : c + w], preferred_element_type=F32)
        up = jnp.dot(rows, wu_ref[0, :, c : c + w], preferred_element_type=F32)
        hidden.append((jax.nn.silu(gate) * up).astype(BF16))
    hidden = jnp.concatenate(hidden, axis=1) if len(hidden) > 1 else hidden[0]
    scale = wcol[...]
    for c, w in column_blocks(width):
        part = jnp.dot(hidden, wd_ref[0, :, c : c + w], preferred_element_type=F32) * scale
        for out, (first, last) in zip(outs, ranges):
            out[:, c : c + w] = part[first:last].astype(out.dtype)


def ffn(scalars, xs, w_gate, w_up, w_down, experts, groups):
    counts = [x.shape[0] for x in xs]
    total = sum(counts)
    width, hidden = w_gate.shape[1:]
    shapes, ranges, done = [], [], 0
    for number, dtype in groups:
        first = sum(counts[:done])
        done += number
        ranges.append((first, sum(counts[:done])))
        shapes.append(jax.ShapeDtypeStruct((ranges[-1][1] - first, width), dtype))
    packed = all(c % 16 == 0 for c in counts)
    return pl.pallas_call(
        functools.partial(ffn_kernel, counts, experts, ranges),
        out_shape=shapes,
        in_specs=[SMEM] + [VMEM] * (len(xs) + 3),
        out_specs=[VMEM] * len(shapes),
        scratch_shapes=[
            pltpu.VMEM((total, width), BF16 if packed else F32),
            pltpu.VMEM((total, 1), F32),
        ],
        compiler_params=params(),
        cost_estimate=cost(6 * total * width * hidden, 6 * width * hidden + 6 * total * width, total * hidden),
    )(scalars, *xs, w_gate, w_up, w_down)


def stage_kernel(*refs):
    count = len(refs) // 2
    sems = refs[-1]
    copies = [pltpu.make_async_copy(refs[i], refs[count + i], sems.at[i]) for i in range(count)]
    for copy in copies:
        copy.start()
    for copy in copies:
        copy.wait()


def stage(weights):
    return pl.pallas_call(
        stage_kernel,
        out_shape=[jax.ShapeDtypeStruct(w.shape, w.dtype) for w in weights],
        in_specs=[HBM] * len(weights),
        out_specs=[VMEM] * len(weights),
        scratch_shapes=[pltpu.SemaphoreType.DMA((len(weights),))],
        compiler_params=params(),
        cost_estimate=cost(0, sum(4 * w.size for w in weights)),
        name="stage",
    )(*weights)


def shared_kernel(x_ref, wg_ref, wu_ref, wd_ref, out_ref):
    step = pl.program_id(0)
    rows = x_ref[...]
    gate = jnp.dot(rows, wg_ref[...], preferred_element_type=F32)
    up = jnp.dot(rows, wu_ref[...], preferred_element_type=F32)
    hidden = (jax.nn.silu(gate) * up).astype(BF16)
    for c, w in column_blocks(rows.shape[1]):
        part = jnp.dot(hidden, wd_ref[:, c : c + w], preferred_element_type=F32)

        @pl.when(step == 0)
        def _():
            out_ref[:, c : c + w] = part

        @pl.when(step > 0)
        def _():
            out_ref[:, c : c + w] += part


def shared(tokens, w_gate, w_up, w_down):
    rows, width = tokens.shape
    hidden = w_gate.shape[1]
    block = hidden_block(hidden)
    return pl.pallas_call(
        shared_kernel,
        grid=(hidden // block,),
        out_shape=jax.ShapeDtypeStruct((rows, width), F32),
        in_specs=[
            pl.BlockSpec((rows, width), lambda f: (0, 0)),
            pl.BlockSpec((width, block), lambda f: (0, f)),
            pl.BlockSpec((width, block), lambda f: (0, f)),
            pl.BlockSpec((block, width), lambda f: (f, 0)),
        ],
        out_specs=pl.BlockSpec((rows, width), lambda f: (0, 0)),
        compiler_params=params(),
        cost_estimate=cost(6 * rows * width * hidden, 6 * width * hidden + 6 * rows * width, rows * hidden),
        name="shared",
    )(tokens, w_gate, w_up, w_down)


def token_blocks(acc, order, s_ref):
    rows = acc.shape[0] // len(order)
    for j, rel in enumerate(order):
        start = pl.multiple_of((s_ref[1] ^ rel) * rows, rows)
        yield j, j * rows, acc[pl.ds(start, rows), :]


def gathered(oh_ref, parts, counts, slots, acc):
    offset = 0
    for ref, count in zip(parts, counts):
        slots[offset : offset + count, :] = ref[...].astype(slots.dtype)
        offset += count
    for c, w in column_blocks(acc.shape[1]):
        acc[:, c : c + w] = lax.dot_general(
            oh_ref[...], slots[:, c : c + w].astype(BF16), (((0,), (0,)), ((), ())), preferred_element_type=F32
        )


def early_kernel(counts, order, s_ref, oh_ref, shared_ref, *refs):
    n = len(counts)
    out_ref, slots, acc = refs[n:]
    gathered(oh_ref, refs[:n], counts, slots, acc)
    acc[...] = acc[...] + shared_ref[...]
    for j, at, value in token_blocks(acc, order, s_ref):
        out_ref[at : at + value.shape[0], :] = value


def combine_kernel(counts, order, s_ref, oh_ref, base_ref, *refs):
    n = len(counts)
    keep_ref, send_ref, slots, acc = refs[n:]
    gathered(oh_ref, refs[:n], counts, slots, acc)
    kept = keep_ref.shape[0]
    for j, at, value in token_blocks(acc, order, s_ref):
        value = value + base_ref[at : at + value.shape[0], :]
        if at < kept:
            keep_ref[at : at + value.shape[0], :] = value
        else:
            send_ref[at - kept : at - kept + value.shape[0], :] = value.astype(BF16)


def combine(scalars, one_hot, base, parts, order, final):
    counts = [p.shape[0] for p in parts]
    tok_rows, width = base.shape
    total = sum(counts)
    packed = all(c % 16 == 0 for c in counts)
    if final:
        shapes = [jax.ShapeDtypeStruct((tok_rows // 2, width), t) for t in (F32, BF16)]
    else:
        shapes = [jax.ShapeDtypeStruct((tok_rows, width), F32)]
    return pl.pallas_call(
        functools.partial(combine_kernel if final else early_kernel, counts, order),
        out_shape=shapes,
        in_specs=[SMEM] + [VMEM] * (len(parts) + 2),
        out_specs=[VMEM] * len(shapes),
        scratch_shapes=[
            pltpu.VMEM((total, width), BF16 if packed else F32),
            pltpu.VMEM((tok_rows, width), F32),
        ],
        compiler_params=params(),
        cost_estimate=cost(2 * total * tok_rows * width, 2 * total * width + 7 * tok_rows * width),
    )(scalars, one_hot, base, *parts)


def fold(value, bits):
    for bit in bits:
        half = value.shape[0] // 2
        value = value[:half] + xor_local(value[half:].astype(BF16), bit).astype(F32)
    return value


def far_chunks(node_count):
    top = node_count // 2
    chunks = []
    while top >= NEAR:
        chunks.append(list(range(top, 2 * top)))
        top //= 2
    if len(chunks) == 1 and len(chunks[0]) > 1:
        ks = chunks[0]
        chunks = [ks[len(ks) // 2 :], ks[: len(ks) // 2]]
    return chunks


def local(tokens, expert_ids, gate_scores, expert_gate, expert_up, expert_down, shared_gate, shared_up, shared_down):
    node_count = lax.axis_size("node")
    local_count = lax.axis_size("local")
    experts = node_count * E_NODE
    tok_rows, _ = tokens.shape
    capacity = expert_ids.shape[1] * tok_rows // (2 * node_count)
    node = lax.axis_index("node")
    rank = lax.axis_index("local")
    own = node * E_NODE + rank // (local_count // E_NODE)
    scalars = jnp.stack([node, rank, own, rank % 2]).astype(jnp.int32)
    slow_bits = [1 << b for b in range(1, local_count.bit_length() - 1)]
    chunks = far_chunks(node_count)
    near = [k for k in range(1, NEAR)]
    pieces = [(k, 1, capacity // local_count) for ks in chunks for k in ks]
    pieces += [(k, 3, capacity // 2) for k in near[1:] + near[:1]] + [(0, None, capacity)]
    in_hbm = functools.partial(pltpu.with_memory_space_constraint, memory_space=pltpu.HBM)
    sends, late_hot, early_hot = route(
        scalars, in_hbm(expert_ids.T), in_hbm(gate_scores.T), in_hbm(tokens), tuple(pieces), node_count
    )
    weights = [pltpu.with_memory_space_constraint(w, pltpu.HBM) for w in (expert_gate, expert_up, expert_down)]
    shared_gate, shared_up, shared_down = [
        pltpu.with_memory_space_constraint(w, pltpu.HBM) for w in (shared_gate, shared_up, shared_down)
    ]

    arrived = []
    index = 0
    for ks in chunks:
        got = []
        for k in ks:
            got.append(xor_node(sends[index], k))
            index += 1
        arrived.append(got)
    near_in = []
    for k in near[1:] + near[:1]:
        near_in.append(xor_node(sends[index], k))
        index += 1
    near_in = near_in[-1:] + near_in[:-1]
    own_rows = sends[-1]

    shared_part = shared(in_hbm(tokens), shared_gate, shared_up, shared_down)
    weights = stage(weights)

    def gather(got):
        rows = [jnp.concatenate(got, axis=0) if len(got) > 1 else got[0]]
        for bit in slow_bits:
            rows = rows + [xor_local(r, bit) for r in rows]
        return rows + [xor_local(r, 1) for r in rows]

    def summed(keep, send):
        return keep + xor_local(send, 1).astype(F32)

    def experts_of(rows):
        half = len(rows) // 2
        keep, send = ffn(scalars, rows, *weights, experts, ((half, F32), (half, BF16)))
        return summed(keep, send)

    partner = xor_local(near_in[0], 1)
    rows = [own_rows, near_in[0], partner]
    own_out, keep, send = ffn(scalars, rows, *weights, experts, ((1, BF16), (1, F32), (1, BF16)))
    near_sum = summed(keep, send).astype(BF16)
    near_back = [xor_node(near_sum, 1)]

    near_rows = near_in[1:] + [xor_local(r, 1) for r in near_in[1:]]
    near_sum = experts_of(near_rows).astype(BF16)
    count = near_sum.shape[0] // len(near_in[1:])
    for i, k in enumerate(near[1:]):
        near_back.append(xor_node(near_sum[i * count : (i + 1) * count], k))
    returned = []
    for ks, got in zip(chunks, arrived):
        value = experts_of(gather(got))
        value = fold(value, slow_bits[::-1]).astype(BF16)
        count = value.shape[0] // len(ks)
        for i, k in enumerate(ks):
            returned.append(xor_node(value[i * count : (i + 1) * count], k))

    order = [0]
    for bit in slow_bits:
        order = order + [i ^ bit for i in order]
    order = order + [i ^ 1 for i in order]
    base = combine(scalars, early_hot, shared_part, [near_back[0], own_out], tuple(order), False)[0]
    parts = returned + near_back[1:]
    keep, send = combine(scalars, late_hot, base, parts, tuple(order), True)
    value = keep + xor_local(send, 1).astype(F32)
    return fold(value, slow_bits[::-1]).astype(BF16)


def solution(mesh):
    return shard(mesh)


def shard(mesh):
    return jax.shard_map(
        local,
        mesh=mesh,
        in_specs=(
            P("node", None),
            P("node", None),
            P("node", None),
            P(("node", "local"), None, None),
            P(("node", "local"), None, None),
            P(("node", "local"), None, None),
            P(None, "local"),
            P(None, "local"),
            P("local", None),
        ),
        out_specs=P(("node", "local"), None),
        check_vma=False,
    )
```

```python
import functools

import jax
import jax.numpy as jnp
from jax import lax
from jax.experimental import pallas as pl
from jax.experimental.pallas import tpu as pltpu
from jax.sharding import PartitionSpec as P


E_NODE = 4
NEAR = 4
LANES = 128
VMEM_LIMIT = 24 * 1024 * 1024
F32 = jnp.float32
BF16 = jnp.bfloat16


def xor_node(x, k):
    count = lax.axis_size("node")
    return lax.ppermute(x, "node", [(i, i ^ k) for i in range(count)])


def xor_local(x, k):
    count = lax.axis_size("local")
    return lax.ppermute(x, "local", [(i, i ^ k) for i in range(count)])


def params():
    return pltpu.CompilerParams(vmem_limit_bytes=VMEM_LIMIT)


def cost(flops, nbytes, trans=0):
    return pl.CostEstimate(flops=int(flops), bytes_accessed=int(nbytes), transcendentals=int(trans))


SMEM = pl.BlockSpec(memory_space=pltpu.SMEM)
HBM = pl.BlockSpec(memory_space=pltpu.HBM)
VMEM = pl.BlockSpec(memory_space=pltpu.VMEM)


def column_blocks(width, block=512):
    return [(c, min(block, width - c)) for c in range(0, width, block)]


def route_kernel(pieces, node_count, s_ref, ids_hbm, score_hbm, tok_hbm, *refs):
    sent = sum(p[4] for p in pieces)
    outs = refs[:sent]
    late_ref, early_ref, hot, rows, ids_ref, score_ref, tok_ref, sems = refs[sent:]
    copies = [
        pltpu.make_async_copy(src, dst, sems.at[i])
        for i, (src, dst) in enumerate(((ids_hbm, ids_ref), (score_hbm, score_ref), (tok_hbm, tok_ref)))
    ]
    for copy in copies:
        copy.start()
    copies[0].wait()
    copies[1].wait()
    tok_rows, width = tok_ref.shape
    picks = ids_ref.shape[0]
    experts = node_count * E_NODE
    node = s_ref[0]
    ids = ids_ref[...]
    group = lax.div(ids, jnp.int32(E_NODE)) ^ node
    score = score_ref[...]
    group_iota = lax.broadcasted_iota(jnp.int32, (node_count, tok_rows), 0)
    expert_iota = lax.broadcasted_iota(jnp.int32, (experts, tok_rows), 0)
    member = jnp.zeros((node_count, tok_rows), F32)
    weight = jnp.zeros((experts, tok_rows), F32)
    for j in range(picks):
        member = jnp.where(group[j : j + 1] == group_iota, 1.0, member)
        weight = weight + jnp.where(ids[j : j + 1] == expert_iota, score[j : j + 1], 0.0)
    row = lax.broadcasted_iota(jnp.int32, (tok_rows, tok_rows), 0)
    col = lax.broadcasted_iota(jnp.int32, (tok_rows, tok_rows), 1)
    upper = jnp.where(row <= col, 1.0, 0.0).astype(BF16)
    position = jnp.dot(member.astype(BF16), upper, preferred_element_type=F32) - 1.0
    position = jnp.where(member > 0.0, position, -1.0).astype(jnp.int32)
    offset = 0
    for k, base, count, rel, _ in pieces:
        first = 0 if base is None else (s_ref[base] ^ rel) * count
        slot = lax.broadcasted_iota(jnp.int32, (count, tok_rows), 0) + first
        hot[offset : offset + count, :] = jnp.where(position[k : k + 1] == slot, 1.0, 0.0)
        offset += count
    one_hot = hot[...].astype(BF16)
    split = late_ref.shape[0]
    late_ref[...] = hot[:split, :].astype(BF16)
    early_ref[...] = hot[split:, :].astype(BF16)
    high = weight.astype(BF16)
    low = (weight - high.astype(F32)).astype(BF16)
    extra = outs[0].shape[1] - width
    parts = [high, low]
    if extra > 2 * experts:
        parts.append(jnp.zeros((extra - 2 * experts, tok_rows), BF16))
    table = jnp.concatenate(parts, axis=0)
    copies[2].wait()
    aligned = all(p[2] % 16 == 0 for p in pieces)
    for c, w in column_blocks(width) + [(width, extra)]:
        if c < width:
            value = jnp.dot(one_hot, tok_ref[:, c : c + w], preferred_element_type=F32)
        else:
            value = lax.dot_general(one_hot, table, (((1,), (1,)), ((), ())), preferred_element_type=F32)
        if not aligned:
            rows[:, :w] = value
            value = rows
        offset, index = 0, 0
        for _, _, count, _, goes in pieces:
            if goes:
                outs[index][:, c : c + w] = value[offset : offset + count, :w].astype(BF16)
                index += 1
            offset += count


def route(scalars, ids, scores, tokens, pieces, node_count):
    tok_rows, width = tokens.shape
    experts = node_count * E_NODE
    full = width + -(-2 * experts // LANES) * LANES
    total = sum(p[2] for p in pieces)
    tail = sum(p[2] for p in pieces[-2:])
    res = pl.pallas_call(
        functools.partial(route_kernel, pieces, node_count),
        out_shape=[jax.ShapeDtypeStruct((p[2], full), BF16) for p in pieces if p[4]]
        + [jax.ShapeDtypeStruct((count, tok_rows), BF16) for count in (total - tail, tail)],
        in_specs=[SMEM, HBM, HBM, HBM],
        out_specs=[VMEM] * (sum(p[4] for p in pieces) + 2),
        scratch_shapes=[
            pltpu.VMEM((total, tok_rows), F32),
            pltpu.VMEM((total, 512), F32),
            pltpu.VMEM(ids.shape, ids.dtype),
            pltpu.VMEM(scores.shape, scores.dtype),
            pltpu.VMEM(tokens.shape, tokens.dtype),
            pltpu.SemaphoreType.DMA((3,)),
        ],
        compiler_params=params(),
        cost_estimate=cost(2 * total * tok_rows * full, 2 * (tok_rows * width + total * full)),
        name="route",
    )(scalars, ids, scores, tokens)
    return res[:-2], res[-2], res[-1]


def hidden_block(hidden):
    for size in (256, 128):
        if hidden % size == 0:
            return size
    return hidden


def ffn_kernel(counts, experts, ranges, s_ref, *refs):
    n = len(counts)
    xs = refs[:n]
    wg_ref, wu_ref, wd_ref = refs[n : n + 3]
    outs = refs[n + 3 : -2]
    x, wcol = refs[-2:]
    _, width = x.shape
    expert = s_ref[2]
    extra = xs[0].shape[1] - width
    lane = lax.broadcasted_iota(jnp.int32, (1, extra), 1)
    mask = jnp.where((lane == expert) | (lane == expert + experts), 1.0, 0.0)
    offset = 0
    for ref, count in zip(xs, counts):
        x[offset : offset + count, :] = ref[:, :width].astype(x.dtype)
        wcol[offset : offset + count, :] = jnp.sum(ref[:, width:].astype(F32) * mask, axis=1, keepdims=True)
        offset += count
    rows = x[...].astype(BF16)
    hidden = []
    for c, w in column_blocks(wg_ref.shape[2], 256):
        gate = jnp.dot(rows, wg_ref[0, :, c : c + w], preferred_element_type=F32)
        up = jnp.dot(rows, wu_ref[0, :, c : c + w], preferred_element_type=F32)
        hidden.append((jax.nn.silu(gate) * up).astype(BF16))
    hidden = jnp.concatenate(hidden, axis=1) if len(hidden) > 1 else hidden[0]
    scale = wcol[...]
    for c, w in column_blocks(width):
        part = jnp.dot(hidden, wd_ref[0, :, c : c + w], preferred_element_type=F32) * scale
        for out, (first, last) in zip(outs, ranges):
            out[:, c : c + w] = part[first:last].astype(out.dtype)


def ffn(scalars, xs, w_gate, w_up, w_down, experts, groups):
    counts = [x.shape[0] for x in xs]
    total = sum(counts)
    width, hidden = w_gate.shape[1:]
    shapes, ranges, done = [], [], 0
    for number, dtype in groups:
        first = sum(counts[:done])
        done += number
        ranges.append((first, sum(counts[:done])))
        shapes.append(jax.ShapeDtypeStruct((ranges[-1][1] - first, width), dtype))
    packed = all(c % 16 == 0 for c in counts)
    return pl.pallas_call(
        functools.partial(ffn_kernel, counts, experts, ranges),
        out_shape=shapes,
        in_specs=[SMEM] + [VMEM] * (len(xs) + 3),
        out_specs=[VMEM] * len(shapes),
        scratch_shapes=[
            pltpu.VMEM((total, width), BF16 if packed else F32),
            pltpu.VMEM((total, 1), F32),
        ],
        compiler_params=params(),
        cost_estimate=cost(6 * total * width * hidden, 6 * width * hidden + 6 * total * width, total * hidden),
    )(scalars, *xs, w_gate, w_up, w_down)


def stage_kernel(*refs):
    count = len(refs) // 2
    sems = refs[-1]
    copies = [pltpu.make_async_copy(refs[i], refs[count + i], sems.at[i]) for i in range(count)]
    for copy in copies:
        copy.start()
    for copy in copies:
        copy.wait()


def stage(weights):
    return pl.pallas_call(
        stage_kernel,
        out_shape=[jax.ShapeDtypeStruct(w.shape, w.dtype) for w in weights],
        in_specs=[HBM] * len(weights),
        out_specs=[VMEM] * len(weights),
        scratch_shapes=[pltpu.SemaphoreType.DMA((len(weights),))],
        compiler_params=params(),
        cost_estimate=cost(0, sum(4 * w.size for w in weights)),
        name="stage",
    )(*weights)


def shared_kernel(x_ref, wg_ref, wu_ref, wd_ref, out_ref):
    step = pl.program_id(0)
    rows = x_ref[...]
    gate = jnp.dot(rows, wg_ref[...], preferred_element_type=F32)
    up = jnp.dot(rows, wu_ref[...], preferred_element_type=F32)
    hidden = (jax.nn.silu(gate) * up).astype(BF16)
    for c, w in column_blocks(rows.shape[1]):
        part = jnp.dot(hidden, wd_ref[:, c : c + w], preferred_element_type=F32)

        @pl.when(step == 0)
        def _():
            out_ref[:, c : c + w] = part

        @pl.when(step > 0)
        def _():
            out_ref[:, c : c + w] += part


def shared(tokens, w_gate, w_up, w_down):
    rows, width = tokens.shape
    hidden = w_gate.shape[1]
    block = hidden_block(hidden)
    return pl.pallas_call(
        shared_kernel,
        grid=(hidden // block,),
        out_shape=jax.ShapeDtypeStruct((rows, width), F32),
        in_specs=[
            pl.BlockSpec((rows, width), lambda f: (0, 0)),
            pl.BlockSpec((width, block), lambda f: (0, f)),
            pl.BlockSpec((width, block), lambda f: (0, f)),
            pl.BlockSpec((block, width), lambda f: (f, 0)),
        ],
        out_specs=pl.BlockSpec((rows, width), lambda f: (0, 0)),
        compiler_params=params(),
        cost_estimate=cost(6 * rows * width * hidden, 6 * width * hidden + 6 * rows * width, rows * hidden),
        name="shared",
    )(tokens, w_gate, w_up, w_down)


def token_blocks(acc, order, s_ref):
    rows = acc.shape[0] // len(order)
    for j, rel in enumerate(order):
        start = pl.multiple_of((s_ref[1] ^ rel) * rows, rows)
        yield j, j * rows, acc[pl.ds(start, rows), :]


def gathered(oh_ref, parts, counts, slots, acc):
    offset = 0
    for ref, count in zip(parts, counts):
        slots[offset : offset + count, :] = ref[...].astype(slots.dtype)
        offset += count
    for c, w in column_blocks(acc.shape[1]):
        acc[:, c : c + w] = lax.dot_general(
            oh_ref[...], slots[:, c : c + w].astype(BF16), (((0,), (0,)), ((), ())), preferred_element_type=F32
        )


def early_kernel(counts, order, s_ref, oh_ref, shared_ref, *refs):
    n = len(counts)
    out_ref, slots, acc = refs[n:]
    gathered(oh_ref, refs[:n], counts, slots, acc)
    acc[...] = acc[...] + shared_ref[...]
    for j, at, value in token_blocks(acc, order, s_ref):
        out_ref[at : at + value.shape[0], :] = value


def combine_kernel(counts, order, s_ref, oh_ref, base_ref, *refs):
    n = len(counts)
    keep_ref, send_ref, slots, acc = refs[n:]
    gathered(oh_ref, refs[:n], counts, slots, acc)
    kept = keep_ref.shape[0]
    for j, at, value in token_blocks(acc, order, s_ref):
        value = value + base_ref[at : at + value.shape[0], :]
        if at < kept:
            keep_ref[at : at + value.shape[0], :] = value
        else:
            send_ref[at - kept : at - kept + value.shape[0], :] = value.astype(BF16)


def combine(scalars, one_hot, base, parts, order, final):
    counts = [p.shape[0] for p in parts]
    tok_rows, width = base.shape
    total = sum(counts)
    packed = all(c % 16 == 0 for c in counts)
    if final:
        shapes = [jax.ShapeDtypeStruct((tok_rows // 2, width), t) for t in (F32, BF16)]
    else:
        shapes = [jax.ShapeDtypeStruct((tok_rows, width), F32)]
    return pl.pallas_call(
        functools.partial(combine_kernel if final else early_kernel, counts, order),
        out_shape=shapes,
        in_specs=[SMEM] + [VMEM] * (len(parts) + 2),
        out_specs=[VMEM] * len(shapes),
        scratch_shapes=[
            pltpu.VMEM((total, width), BF16 if packed else F32),
            pltpu.VMEM((tok_rows, width), F32),
        ],
        compiler_params=params(),
        cost_estimate=cost(2 * total * tok_rows * width, 2 * total * width + 7 * tok_rows * width),
    )(scalars, one_hot, base, *parts)


def fold(value, bits):
    for bit in bits:
        half = value.shape[0] // 2
        value = value[:half] + xor_local(value[half:].astype(BF16), bit).astype(F32)
    return value


def far_chunks(node_count):
    top = node_count // 2
    chunks = []
    while top >= NEAR:
        chunks.append(list(range(top, 2 * top)))
        top //= 2
    if len(chunks) == 1 and len(chunks[0]) > 1:
        ks = chunks[0]
        chunks = [ks[len(ks) // 2 :], ks[: len(ks) // 2]]
    return chunks


def local(tokens, expert_ids, gate_scores, expert_gate, expert_up, expert_down, shared_gate, shared_up, shared_down):
    node_count = lax.axis_size("node")
    local_count = lax.axis_size("local")
    experts = node_count * E_NODE
    tok_rows, _ = tokens.shape
    capacity = expert_ids.shape[1] * tok_rows // (2 * node_count)
    node = lax.axis_index("node")
    rank = lax.axis_index("local")
    own = node * E_NODE + rank // (local_count // E_NODE)
    scalars = jnp.stack([node, rank, own, rank % 2]).astype(jnp.int32)
    slow_bits = [1 << b for b in range(1, local_count.bit_length() - 1)]
    chunks = far_chunks(node_count)
    near = [k for k in range(1, NEAR)]
    whole_k = chunks[0][-1]
    slow = [0]
    for bit in slow_bits:
        slow = slow + [i ^ bit for i in slow]
    pieces = []
    for k in (k for ks in chunks for k in ks):
        rels = slow if k == whole_k else slow[:1]
        pieces += [(k, 1, capacity // local_count, rel, rel == 0) for rel in rels]
    pieces += [(k, 3, capacity // 2, 0, True) for k in near[1:] + near[:1]] + [(0, None, capacity, 0, True)]
    in_hbm = functools.partial(pltpu.with_memory_space_constraint, memory_space=pltpu.HBM)
    sends, late_hot, early_hot = route(
        scalars, in_hbm(expert_ids.T), in_hbm(gate_scores.T), in_hbm(tokens), tuple(pieces), node_count
    )
    weights = [pltpu.with_memory_space_constraint(w, pltpu.HBM) for w in (expert_gate, expert_up, expert_down)]
    shared_gate, shared_up, shared_down = [
        pltpu.with_memory_space_constraint(w, pltpu.HBM) for w in (shared_gate, shared_up, shared_down)
    ]

    arrived = []
    index = 0
    for ks in chunks:
        got = []
        for k in ks:
            got.append(xor_node(sends[index], k))
            index += 1
        arrived.append(got)
    near_in = []
    for k in near[1:] + near[:1]:
        near_in.append(xor_node(sends[index], k))
        index += 1
    near_in = near_in[-1:] + near_in[:-1]
    own_rows = sends[-1]

    shared_part = shared(in_hbm(tokens), shared_gate, shared_up, shared_down)
    weights = stage(weights)

    def gather(got):
        rows = [jnp.concatenate(got, axis=0) if len(got) > 1 else got[0]]
        for bit in slow_bits:
            rows = rows + [xor_local(r, bit) for r in rows]
        return rows + [xor_local(r, 1) for r in rows]

    def summed(keep, send):
        return keep + xor_local(send, 1).astype(F32)

    def experts_of(rows):
        half = len(rows) // 2
        keep, send = ffn(scalars, rows, *weights, experts, ((half, F32), (half, BF16)))
        return summed(keep, send)

    partner = xor_local(near_in[0], 1)
    rows = [own_rows, near_in[0], partner]
    own_out, keep, send = ffn(scalars, rows, *weights, experts, ((1, BF16), (1, F32), (1, BF16)))
    near_sum = summed(keep, send).astype(BF16)
    near_back = [xor_node(near_sum, 1)]

    near_rows = near_in[1:] + [xor_local(r, 1) for r in near_in[1:]]
    near_sum = experts_of(near_rows).astype(BF16)
    count = near_sum.shape[0] // len(near_in[1:])
    for i, k in enumerate(near[1:]):
        near_back.append(xor_node(near_sum[i * count : (i + 1) * count], k))
    returned = []
    for ks, got in zip(chunks, arrived):
        value = experts_of(gather(got))
        count = capacity // local_count
        back = {}
        if whole_k in ks:
            runs = [value[i : i + len(ks) * count] for i in range(0, value.shape[0], len(ks) * count)]
            cut = ks.index(whole_k) * count
            whole = jnp.concatenate([r[cut : cut + count] for r in runs], axis=0).astype(BF16)
            back[whole_k] = xor_node(whole, whole_k)
            value = jnp.concatenate([r[:cut] for r in runs], axis=0)
        rest = [k for k in ks if k != whole_k]
        value = fold(value, slow_bits[::-1]).astype(BF16)
        for i, k in enumerate(rest):
            back[k] = xor_node(value[i * count : (i + 1) * count], k)
        returned += [back[k] for k in ks]

    order = [0]
    for bit in slow_bits:
        order = order + [i ^ bit for i in order]
    order = order + [i ^ 1 for i in order]
    base = combine(scalars, early_hot, shared_part, [near_back[0], own_out], tuple(order), False)[0]
    parts = returned + near_back[1:]
    keep, send = combine(scalars, late_hot, base, parts, tuple(order), True)
    value = keep + xor_local(send, 1).astype(F32)
    return fold(value, slow_bits[::-1]).astype(BF16)


def solution(mesh):
    return shard(mesh)


def shard(mesh):
    return jax.shard_map(
        local,
        mesh=mesh,
        in_specs=(
            P("node", None),
            P("node", None),
            P("node", None),
            P(("node", "local"), None, None),
            P(("node", "local"), None, None),
            P(("node", "local"), None, None),
            P(None, "local"),
            P(None, "local"),
            P("local", None),
        ),
        out_specs=P(("node", "local"), None),
        check_vma=False,
    )
```
